32 devices in a mesh: grp: 4 (over z), tok: 8 (over y, x, core).
Axes of the slice: x: 2, y: 2, z: 4, core: 2. Of those that a mesh axis runs over, the one named last changes fastest.
Arguments:
- tokens: bfloat16 [8192, 2048], P(('grp', 'tok')), may hold values from -6 to 6
- cotangent: bfloat16 [8192, 2048], P(('grp', 'tok')), may hold values from -6 to 6
- norm_gain: bfloat16 [2048], P(('grp', 'tok')), may hold values from 0.099609375 to 1.8984375
- norm_bias: bfloat16 [2048], P(('grp', 'tok')), may hold values from -3 to 3
- joint_weight: bfloat16 [2048, 6144], P(('grp', 'tok')), may hold values from -0.125 to 0.125
- out_weight: bfloat16 [2048, 2048], P(('grp', 'tok')), may hold values from -2 to 2
- gate_weight: bfloat16 [2048, 5632], P(('grp', 'tok')), may hold values from -0.125 to 0.125
- up_weight: bfloat16 [2048, 5632], P(('grp', 'tok')), may hold values from -0.125 to 0.125
- down_weight: bfloat16 [5632, 2048], P(('grp', 'tok')), may hold values from -0.078125 to 0.078125
- block_table: int32 [4, 16], P('grp'), may hold values from 0 to 15, each once within a row
Outputs:
- result: bfloat16 [8192, 2048], P(('grp', 'tok'))
- input_grad: bfloat16 [8192, 2048], P(('grp', 'tok'))
- gain_grad: float32 [2048], P(('grp', 'tok'))
- bias_grad: float32 [2048], P(('grp', 'tok'))
- joint_grad: float32 [2048, 6144], P(('grp', 'tok'))
- out_grad: float32 [2048, 2048], P(('grp', 'tok'))
- gate_grad: float32 [2048, 5632], P(('grp', 'tok'))
- up_grad: float32 [2048, 5632], P(('grp', 'tok'))
- down_grad: float32 [5632, 2048], P(('grp', 'tok'))
The draws below stay inside these ranges and needn't reach their ends.
Inputs may be any that keep to these rules, and one draw needn't show every extreme that they name: Each row of block_table is a permutation; value v in a slot of grp index r places there block v % 16 of group v // 16 of that index: a prompt block if v % 16 < 8, else one continuation.
All inputs are finite; a program needn't handle non-finite values.
Results may differ from the reference program's by a relative error of at most 0.012.
Values may be sent and summed in bfloat16 or wider, within the bound.
No kernel may reach another device: no remote copies, remote signals or barrier semaphores. Data moves between devices by JAX's collectives and lax.ppermute only.
A program may use at most 640 MiB of HBM per device.

```python
import jax
import jax.numpy as jnp
from jax import lax

D = 2048
HEADS = 32
HD = 64
ROT = 16
FF = 5632
BT = 128
PB = 8
BLK_GROUP = 16
BR = 16
ROW_TOK = 2048
ROWS = 4
TOKENS = 8192
PROMPT = 1024


def with_spikes(values, rng, source, target, shards_of, factor):
    owner, partner = [(jnp.arange(values.shape[dim]) // (values.shape[dim] // shards_of)).reshape([-1 if axis == dim else 1 for axis in range(values.ndim)]) for dim in (source, target)]
    chosen = jax.random.permutation(rng, shards_of)[partner]
    strong = (owner == chosen) | (owner == (partner + shards_of // 2) % shards_of)
    return jnp.where(strong, factor * values, values)


def block_levels(rng, shape, cuts, smallest, largest):
    def one(dim, parts):
        draws = jax.random.uniform(jax.random.fold_in(jax.random.fold_in(rng, 6), dim), (parts,), jnp.float32, smallest / len(cuts), largest / len(cuts))
        return jnp.repeat(jnp.exp(draws), shape[dim] // parts).reshape((-1,) + (1,) * (len(shape) - dim - 1))

    level = one(*cuts[0])
    for cut in cuts[1:]:
        level = level * one(*cut)
    return level


def scatter_about(stream_key, shape, deviation, bound, cuts=(), kind=jnp.bfloat16):
    loudness = block_levels(stream_key, shape, cuts, -0.22, 0.18) if cuts else 1.0
    array = jax.random.normal(stream_key, shape, jnp.float32) * deviation * loudness
    return jnp.minimum(jnp.maximum(array, -bound), bound).astype(kind)


def heavy_noise(rng, shape, scale, limit, cuts, heavy, held_as=jnp.bfloat16):
    values = scale * jax.random.normal(rng, shape, jnp.float32)
    if cuts:
        values = values * block_levels(rng, shape, cuts, -0.22, 0.18)
    return jnp.clip(with_spikes(values, jax.random.fold_in(rng, 3), *heavy), -limit, limit).astype(held_as)


def setup_inputs(seed: int = 0) -> dict:
    keys = jax.random.split(jax.random.key(seed), 11)
    tokens = heavy_noise(keys[0], (TOKENS, D), 1.0, 6.0, ((0, 32),), (0, 1, 32, 2.75))
    cotangent = scatter_about(keys[1], (TOKENS, D), 1.0, 6.0, ((0, 32),))
    norm_gain = jnp.clip(1.0 + 0.18 * jax.random.normal(keys[2], (D,), jnp.float32), 0.099609375, 1.8984375).astype(jnp.bfloat16)
    norm_bias = scatter_about(keys[3], (D,), 0.5, 3.0, ((0, 32),))
    joint_weight = scatter_about(keys[4], (D, 3 * D), D ** -0.5, 0.125, ((0, 32),))
    out_weight = scatter_about(keys[5], (D, D), 8 ** -0.5, 2.0, ((0, 32),))
    gate_weight = scatter_about(keys[6], (D, FF), D ** -0.5, 0.125, ((0, 32),))
    up_weight = scatter_about(keys[7], (D, FF), D ** -0.5, 0.125, ((0, 32),))
    down_weight = scatter_about(keys[8], (FF, D), FF ** -0.5, 0.078125, ((0, 32),))
    block_table = jax.vmap(lambda own: jax.random.permutation(own, BR))(jax.random.split(keys[9], ROWS)).reshape((ROWS, BR)).astype(jnp.int32)
    return {"tokens": tokens, "cotangent": cotangent, "norm_gain": norm_gain, "norm_bias": norm_bias, "joint_weight": joint_weight, "out_weight": out_weight, "gate_weight": gate_weight, "up_weight": up_weight, "down_weight": down_weight, "block_table": block_table}


@jax.custom_vjp
def low(v):
    return lax.optimization_barrier(v.astype(jnp.bfloat16)).astype(jnp.float32)

@jax.custom_vjp
def low_back(v):
    return v

def low_keep(v):
    return (low(v), None)

def low_pass(kept, grad):
    return (grad,)

def back_keep(v):
    return (v, None)

def back_low(kept, grad):
    return (low(grad),)
low.defvjp(low_keep, low_pass)
low_back.defvjp(back_keep, back_low)
eps = 1e-05
neg_big = -1e+30

def product(left, right):
    return jnp.dot(left, right, precision=lax.Precision.HIGHEST, preferred_element_type=jnp.float32)

def spread_blocks(values):
    return jnp.repeat(values, BT, axis=-1)

def token_tables(block_table):
    part_of = (block_table % BLK_GROUP).astype(jnp.int32)
    group_of = (block_table // BLK_GROUP).astype(jnp.int32)
    is_prompt = part_of < PB
    begins = jnp.where(is_prompt, part_of * BT, PROMPT).astype(jnp.int32)
    offsets = jnp.arange(BT, dtype=jnp.int32)
    position = (begins[..., None] + offsets).reshape(block_table.shape[:-1] + (-1,)).astype(jnp.int32)
    return (position, spread_blocks(group_of), spread_blocks(part_of), spread_blocks(is_prompt))

def permitted(query_info, key_info):
    q_pos, q_grp, q_part = query_info
    k_pos, k_grp, k_part, k_prompt = key_info
    same = q_grp[:, None] == k_grp[None, :]
    causal = k_pos[None, :] <= q_pos[:, None]
    either = k_prompt[None, :] | (k_part[None, :] == q_part[:, None])
    return same & causal & either

def frequencies():
    return 10000.0 ** (-jnp.arange(0, ROT, 2, dtype=jnp.float32) / ROT)

def turn(values, cosine, sine):
    half = ROT // 2
    first = values[..., :half]
    second = values[..., half:ROT]
    return jnp.concatenate([first * cosine - second * sine, second * cosine + first * sine, values[..., ROT:]], axis=-1)

def block_attention(query, key, value, q_pos, q_grp, q_part, k_pos, k_grp, k_part, k_prompt):
    raw = jnp.einsum('qhd,khd->hqk', query, key, precision=lax.Precision.HIGHEST) * HD ** (-0.5)
    scores = low_back(raw)
    allowed = permitted((q_pos, q_grp, q_part), (k_pos, k_grp, k_part, k_prompt))
    weights = jax.nn.softmax(jnp.where(allowed[None], scores, neg_big), axis=-1)
    weights = low(weights)
    return jnp.einsum('hqk,khd->qhd', weights, value, precision=lax.Precision.HIGHEST)
checked_block = jax.checkpoint(block_attention)

def attend(query, key, value, tables):
    width_q = min(512, ROW_TOK)
    count_q = ROW_TOK // width_q

    def per_row(item):
        q_row, k_row, v_row, k_pos, k_grp, k_part, k_prompt = item

        def per_block(piece):
            q_piece, q_pos, q_grp, q_part = piece
            return checked_block(q_piece, k_row, v_row, q_pos, q_grp, q_part, k_pos, k_grp, k_part, k_prompt)
        pieces = (q_row.reshape(count_q, width_q, HEADS, HD), k_pos.reshape(count_q, width_q), k_grp.reshape(count_q, width_q), k_part.reshape(count_q, width_q))
        return lax.map(per_block, pieces).reshape(ROW_TOK, HEADS, HD)
    return lax.map(per_row, (query, key, value) + tables)

def forward(inputs, gain, bias, joint_w, out_w, gate_w, up_w, down_w, tables):
    mean = lax.optimization_barrier(jnp.mean(inputs, axis=-1, keepdims=True))
    centred = inputs - mean
    inv_std = lax.rsqrt(lax.optimization_barrier(jnp.mean(centred * centred, axis=-1, keepdims=True)) + eps)
    normed = centred * inv_std
    hidden_in = low(normed * gain + bias)
    joint = low_back(product(hidden_in, joint_w))
    position = tables[0].reshape(TOKENS)
    angles = position.astype(jnp.float32)[:, None] * frequencies()[None, :]
    cosine = jnp.cos(angles)[:, None, :]
    sine = jnp.sin(angles)[:, None, :]
    query = low(turn(joint[:, :D].reshape(TOKENS, HEADS, HD), cosine, sine))
    key = low(turn(joint[:, D:2 * D].reshape(TOKENS, HEADS, HD), cosine, sine))
    value = low(joint[:, 2 * D:]).reshape(TOKENS, HEADS, HD)
    shape_rows = (ROWS, ROW_TOK, HEADS, HD)
    attended = attend(query.reshape(shape_rows), key.reshape(shape_rows), value.reshape(shape_rows), tables)
    attended = low(low_back(attended.reshape(TOKENS, D)))
    gate = low_back(product(hidden_in, gate_w))
    up = low_back(product(hidden_in, up_w))
    activated = low(jax.nn.silu(gate) * up)
    return inputs + product(attended, out_w) + product(activated, down_w)

def reference(tokens, cotangent, norm_gain, norm_bias, joint_weight, out_weight, gate_weight, up_weight, down_weight, block_table):
    tables = token_tables(block_table)
    primals = tuple((a.astype(jnp.float32) for a in (tokens, norm_gain, norm_bias, joint_weight, out_weight, gate_weight, up_weight, down_weight)))

    def run(*values):
        return forward(*values, tables)
    output, pull = jax.vjp(run, *primals)
    grads = pull(cotangent.astype(jnp.float32))
    return (output.astype(jnp.bfloat16), grads[0].astype(jnp.bfloat16), grads[1], grads[2], grads[3], grads[4], grads[5], grads[6], grads[7])
```

```python
import functools

import jax
import jax.numpy as jnp
from jax import lax
from jax.experimental import pallas as pl
from jax.experimental.pallas import tpu as pltpu
from jax.sharding import PartitionSpec as P

HD = 64
ROT = 16
BT = 128
PB = 8
BLK_GROUP = 16
LANES = 128
QT = 2 * BT

eps = 1e-05
neg_big = -1e30
bf16 = jnp.bfloat16
f32 = jnp.float32
both = ("grp", "tok")
no_cost = pl.CostEstimate(flops=0, transcendentals=0, bytes_accessed=0)


def matmul(left, right):
    return jnp.dot(left, right, preferred_element_type=f32)


def matmul_nt(left, right):
    return lax.dot_general(left, right, (((1,), (1,)), ((), ())), preferred_element_type=f32)


def matmul_tn(left, right):
    return lax.dot_general(left, right, (((0,), (0,)), ((), ())), preferred_element_type=f32)


def rotary_tables():
    positions = (PB + 1) * BT
    freq = 10000.0 ** (-jnp.arange(0, ROT, 2, dtype=f32) / ROT)
    angles = jnp.arange(positions, dtype=jnp.int32).astype(f32)[:, None] * freq[None, :]
    cosine, sine = jnp.cos(angles), jnp.sin(angles)
    rest = jnp.zeros((positions, HD - ROT), f32)
    none = jnp.zeros_like(sine)

    def widen(parts):
        one = jnp.concatenate(parts, axis=1)
        return jnp.concatenate([one] * (LANES // HD), axis=1)

    keep = widen([cosine, cosine, rest + 1.0])
    below = widen([-sine, none, rest])
    above = widen([none, sine, rest])
    return keep, below, above


def attention_kernel(
    place, joint, d_out, keep, below, above, out, d_joint, qs, ks, vs, ds, d_key, d_value
):
    head = pl.program_id(0)
    half = head % 2
    lane_block = head // 2
    span = d_out.shape[1]
    lanes = [pl.ds(pl.multiple_of(c * span + lane_block * LANES, LANES), LANES) for c in range(3)]
    mine = lax.broadcasted_iota(jnp.int32, (BT, LANES), 1) // HD == half

    def turned(values, part, sign):
        row = min(part, PB) * BT
        c, b, a = (t[row : row + BT, :] for t in (keep, below, above))
        up = pltpu.roll(values, LANES - ROT // 2, 1)
        down = pltpu.roll(values, ROT // 2, 1)
        return values * c + sign * (up * b + down * a)

    def rows_of(part):
        return pl.ds(pl.multiple_of(place[part] * BT, BT), BT)

    for part in range(BLK_GROUP):
        rows = rows_of(part)
        here = pl.ds(part * BT, BT)
        query = turned(joint[rows, lanes[0]], part, 1.0).astype(bf16) * HD ** (-0.5)
        key = turned(joint[rows, lanes[1]], part, 1.0).astype(bf16)
        qs[here, :] = jnp.where(mine, query, 0).astype(bf16)
        ks[here, :] = jnp.where(mine, key, 0).astype(bf16)
        vs[here, :] = jnp.where(mine, joint[rows, lanes[2]].astype(bf16), 0).astype(bf16)
        ds[here, :] = jnp.where(mine, d_out[rows, lanes[0]], 0).astype(bf16)
    d_key[...] = jnp.zeros_like(d_key)
    d_value[...] = jnp.zeros_like(d_value)

    def put(ref, rows, where, values):
        @pl.when(half == 0)
        def _():
            ref[rows, where] = values

        @pl.when(half != 0)
        def _():
            ref[rows, where] = jnp.where(mine, values, ref[rows, where]).astype(ref.dtype)

    row_id = lax.broadcasted_iota(jnp.int32, (QT, QT), 0)
    col_id = lax.broadcasted_iota(jnp.int32, (QT, QT), 1)
    causal = row_id >= col_id
    alone = causal & (row_id // BT == col_id // BT)

    def tile(index, shared, allowed):
        start = index * QT
        own = pl.ds(start, QT)
        query, d_o = qs[own, :], ds[own, :]
        spans = [own] + ([pl.ds(0, shared)] if shared else [])
        raw = [matmul_nt(query, ks[s, :]) for s in spans]
        raw[0] = jnp.where(allowed, raw[0], neg_big)
        top = functools.reduce(jnp.maximum, [jnp.max(r, axis=1, keepdims=True) for r in raw])
        terms = [jnp.exp(r - top) for r in raw]
        total = functools.reduce(jnp.add, [jnp.sum(t, axis=1, keepdims=True) for t in terms])
        inverse = 1.0 / total
        weights = [t * inverse for t in terms]
        low = [w.astype(bf16) for w in weights]
        attended = functools.reduce(jnp.add, [matmul(w, vs[s, :]) for w, s in zip(low, spans)])
        delta = jnp.sum(attended * d_o.astype(f32), axis=1, keepdims=True)
        d_scores = [
            (w * (matmul_nt(d_o, vs[s, :]) - delta)).astype(bf16) for w, s in zip(weights, spans)
        ]
        d_query = functools.reduce(jnp.add, [matmul(d, ks[s, :]) for d, s in zip(d_scores, spans)])
        d_query = d_query * HD ** (-0.5)
        for s, d, w in zip(spans, d_scores, low):
            d_key[s, :] += matmul_tn(d, query)
            d_value[s, :] += matmul_tn(w, d_o)
        for k in range(QT // BT):
            part = index * (QT // BT) + k
            rows = rows_of(part)
            piece = slice(k * BT, (k + 1) * BT)
            put(out, rows, lanes[0], attended[piece, :].astype(bf16))
            put(d_joint, rows, lanes[0], turned(d_query[piece, :], part, -1.0).astype(bf16))

    prompt_tiles = PB * BT // QT
    for index in range(BLK_GROUP * BT // QT):
        if index < prompt_tiles:
            tile(index, index * QT, causal)
        else:
            tile(index, PB * BT, alone)
    for part in range(BLK_GROUP):
        here = pl.ds(part * BT, BT)
        rows = rows_of(part)
        put(d_joint, rows, lanes[1], turned(d_key[here, :], part, -1.0).astype(bf16))
        put(d_joint, rows, lanes[2], d_value[here, :].astype(bf16))


def attention(place, joint, d_out, tables):
    count, span = d_out.shape
    full = lambda shape: pl.BlockSpec(shape, lambda h, p: (0,) * len(shape))
    scratch = [pltpu.VMEM((count, LANES), bf16)] * 4 + [pltpu.VMEM((count, LANES), f32)] * 2
    return pl.pallas_call(
        attention_kernel,
        grid_spec=pltpu.PrefetchScalarGridSpec(
            num_scalar_prefetch=1,
            grid=(span // HD,),
            in_specs=[full(joint.shape), full(d_out.shape)] + [full(t.shape) for t in tables],
            out_specs=[full((count, span)), full((count, 3 * span))],
            scratch_shapes=scratch,
        ),
        out_shape=[
            jax.ShapeDtypeStruct((count, span), bf16),
            jax.ShapeDtypeStruct((count, 3 * span), bf16),
        ],
        compiler_params=pltpu.CompilerParams(vmem_limit_bytes=48 * 2**20),
        cost_estimate=no_cost,
    )(place, joint, d_out, *tables)


def after(values, *earlier):
    return lax.optimization_barrier((values, earlier))[0]


def gather_pieces(values):
    toks = lax.axis_size("tok")
    bits = toks.bit_length() - 1
    paths = values.shape[0] // BT
    orders = [list(range(1, bits)) + [0], list(range(bits - 1, 0, -1)) + [0]]
    held = list(jnp.split(values, paths))
    found = []
    for step in range(bits):
        swaps = [[(i, i ^ (1 << orders[p % 2][step])) for i in range(toks)] for p in range(paths)]
        got = [lax.ppermute(h, "tok", s) for h, s in zip(held, swaps)]
        if step == bits - 1:
            found = [piece for pair in zip(held, got) for piece in pair]
        else:
            held = [jnp.concatenate(pair) for pair in zip(held, got)]
    return found, orders[:paths]


def order_of(orders):
    found = []
    for half, order in enumerate(orders):
        for q in range(1 << len(order)):
            found.append((sum(1 << b for k, b in enumerate(order) if q >> k & 1), half))
    return found


def assemble_kernel(count, norm, *refs):
    pieces, refs = refs[:count], refs[count:]
    step = pl.program_id(0)
    each = pl.num_programs(0) // count
    for k, piece in enumerate(pieces):

        @pl.when(step // each == k)
        def _():
            if norm:
                gain, bias, out = refs
                values = piece[...].astype(f32)
                centred = values - jnp.mean(values, axis=-1, keepdims=True)
                spread = jnp.mean(centred * centred, axis=-1, keepdims=True)
                out[...] = (centred * lax.rsqrt(spread + eps) * gain[...] + bias[...]).astype(bf16)
            else:
                refs[-1][...] = piece[...]


def assemble(pieces, *norm):
    tall, width = pieces[0].shape
    block = min(tall, QT)
    each = tall // block
    total = tall * len(pieces)

    def piece_block(k):
        return pl.BlockSpec((block, width), lambda i: (jnp.clip(i - k * each, 0, each - 1), 0))

    return pl.pallas_call(
        functools.partial(assemble_kernel, len(pieces), bool(norm)),
        grid=(total // block,),
        in_specs=[piece_block(k) for k in range(len(pieces))]
        + [pl.BlockSpec((1, width), lambda i: (0, 0)) for _ in norm],
        out_specs=pl.BlockSpec((block, width), lambda i: (i, 0)),
        out_shape=jax.ShapeDtypeStruct((total, width), bf16),
        compiler_params=pltpu.CompilerParams(vmem_limit_bytes=48 * 2**20),
        cost_estimate=no_cost,
    )(*pieces, *norm)


def sum_kernel(count, transposed, *refs):
    product = matmul_nt if transposed else matmul
    terms = [product(refs[k][...], refs[count + k][...]) for k in range(count)]
    refs[-1][...] = functools.reduce(jnp.add, terms).astype(bf16)


def sum_of_products(lefts, rights, transposed):
    rows = lefts[0].shape[0]
    cols = rights[0].shape[0 if transposed else 1]
    inner = sum(v.shape[1] for v in lefts)
    block = QT
    return pl.pallas_call(
        functools.partial(sum_kernel, len(lefts), transposed),
        grid=(rows // block,),
        in_specs=[pl.BlockSpec((block, v.shape[1]), lambda i: (i, 0)) for v in lefts]
        + [pl.BlockSpec(v.shape, lambda i: (0, 0), pipeline_mode=pl.Buffered(1)) for v in rights],
        out_specs=pl.BlockSpec((block, cols), lambda i: (i, 0)),
        out_shape=jax.ShapeDtypeStruct((rows, cols), bf16),
        compiler_params=pltpu.CompilerParams(vmem_limit_bytes=48 * 2**20),
        cost_estimate=no_cost,
    )(*lefts, *rights)


def feed_kernel(hidden, d_result, up_weight, down_weight, act, d_both):
    wide = act.shape[1]
    both_here = matmul(hidden[...], up_weight[...])
    d_act = matmul_nt(d_result[...], down_weight[...])
    gate, up = both_here[:, :wide], both_here[:, wide:]
    sigma = jax.nn.sigmoid(gate)
    swish = gate * sigma
    act[...] = (swish * up).astype(bf16)
    d_gate = d_act * up * sigma * (1.0 + gate * (1.0 - sigma))
    d_both[...] = jnp.concatenate([d_gate, d_act * swish], axis=1).astype(bf16)


def feed_forward(hidden, d_result, up_weight, down_weight):
    rows, width = hidden.shape
    wide = down_weight.shape[0]
    fixed = lambda w: pl.BlockSpec(w.shape, lambda i: (0, 0), pipeline_mode=pl.Buffered(1))
    return pl.pallas_call(
        feed_kernel,
        grid=(rows // QT,),
        in_specs=[pl.BlockSpec((QT, width), lambda i: (i, 0))] * 2
        + [fixed(up_weight), fixed(down_weight)],
        out_specs=[
            pl.BlockSpec((QT, wide), lambda i: (i, 0)),
            pl.BlockSpec((QT, 2 * wide), lambda i: (i, 0)),
        ],
        out_shape=[
            jax.ShapeDtypeStruct((rows, wide), bf16),
            jax.ShapeDtypeStruct((rows, 2 * wide), bf16),
        ],
        compiler_params=pltpu.CompilerParams(vmem_limit_bytes=48 * 2**20),
        cost_estimate=no_cost,
    )(hidden, d_result, up_weight, down_weight)


def outer_kernel(left, right, out):
    out[...] = matmul_tn(left[...], right[...]).astype(bf16)


def outer_product(left, right):
    rows, tall = left.shape
    wide = right.shape[1]
    return pl.pallas_call(
        outer_kernel,
        grid=(tall // QT,),
        in_specs=[
            pl.BlockSpec((rows, QT), lambda i: (0, i)),
            pl.BlockSpec((rows, wide), lambda i: (0, 0), pipeline_mode=pl.Buffered(1)),
        ],
        out_specs=pl.BlockSpec((QT, wide), lambda i: (i, 0)),
        out_shape=jax.ShapeDtypeStruct((tall, wide), bf16),
        compiler_params=pltpu.CompilerParams(vmem_limit_bytes=48 * 2**20),
        cost_estimate=no_cost,
    )(left, right)


def scatter_pieces(values, orders):
    toks = lax.axis_size("tok")
    bits = toks.bit_length() - 1
    held = list(jnp.split(values, len(orders)))
    for step in range(bits - 1, -1, -1):
        sent = [h[h.shape[0] // 2 :] for h in held]
        swaps = [[(i, i ^ (1 << order[step])) for i in range(toks)] for order in orders]
        got = [lax.ppermute(v, "tok", w) for v, w in zip(sent, swaps)]
        held = [
            h[: h.shape[0] // 2].astype(f32) + g.astype(f32) for h, g in zip(held, got)
        ]
        if step:
            held = [h.astype(bf16) for h in held]
    return jnp.concatenate(held)


def gather_grp(values):
    return lax.all_gather(values, "grp", axis=0, tiled=True)


def scatter_grp(values):
    return lax.psum_scatter(values.astype(bf16), "grp", scatter_dimension=0, tiled=True)


def swap_tok(values):
    return lax.all_to_all(values, "tok", 0, 0)


def split_kernel(outer, *refs):
    sources, out = refs[:-1], refs[-1]
    toks = out.shape[0]
    for tok in range(toks):
        pieces = []
        for source in sources:
            inner = source.shape[1] // (outer * toks)
            values = source[...]
            for k in range(outer):
                start = (k * toks + tok) * inner
                pieces.append(values[:, start : start + inner])
        out[tok] = jnp.concatenate(pieces, axis=1)


def split_columns(weights, outer, toks):
    rows = weights[0].shape[0]
    cols = sum(w.shape[1] for w in weights) // toks
    return pl.pallas_call(
        functools.partial(split_kernel, outer),
        out_shape=jax.ShapeDtypeStruct((toks, rows, cols), weights[0].dtype),
        compiler_params=pltpu.CompilerParams(vmem_limit_bytes=32 * 2**20),
    )(*weights)


def join_kernel(outer, source, *outs):
    toks = source.shape[0]
    offset = 0
    for out in outs:
        inner = out.shape[1] // (outer * toks)
        pieces = []
        for k in range(outer):
            for tok in range(toks):
                start = offset + k * inner
                pieces.append(source[tok, :, start : start + inner].astype(f32))
        out[...] = jnp.concatenate(pieces, axis=1)
        offset += outer * inner


def join_columns(parts, outer, count):
    toks, rows, cols = parts.shape
    shape = jax.ShapeDtypeStruct((rows, toks * cols // count), f32)
    return pl.pallas_call(
        functools.partial(join_kernel, outer),
        out_shape=[shape] * count,
        compiler_params=pltpu.CompilerParams(vmem_limit_bytes=32 * 2**20),
    )(parts)


def body(
    tokens,
    cotangent,
    norm_gain,
    norm_bias,
    joint_weight,
    out_weight,
    gate_weight,
    up_weight,
    down_weight,
    block_table,
):
    grps, toks = lax.axis_size("grp"), lax.axis_size("tok")
    devices = grps * toks
    rows, width = tokens.shape
    own_heads = width // HD // toks
    span = own_heads * HD
    wide = gate_weight.shape[1] // toks
    tok = lax.axis_index("tok")

    pair = jnp.stack([norm_gain, norm_bias])
    pair = lax.all_to_all(jnp.broadcast_to(pair[None], (devices,) + pair.shape), both, 0, 0)
    gain = pair[:, 0].reshape(width).astype(f32)
    bias = pair[:, 1].reshape(width).astype(f32)

    whole_heads = out_weight.shape[0] == HD
    if whole_heads:
        first = gather_grp(jnp.concatenate([down_weight, out_weight]))
        first = first.reshape(grps, -1, width)
        down_w = first[:, : down_weight.shape[0]].reshape(-1, width)
        out_w = first[:, down_weight.shape[0] :].reshape(-1, width)
    else:
        down_w = first = gather_grp(down_weight)
        out_w = lax.all_gather(out_weight, both, axis=0, tiled=True)
        out_w = lax.dynamic_index_in_dim(
            out_w.reshape(own_heads, toks, HD, width), tok, 1, keepdims=False
        ).reshape(span, width)
    gate_up_own = swap_tok(split_columns([gate_weight, up_weight], grps, toks))
    gate_up_w = gather_grp(after(gate_up_own.reshape(-1, 2 * wide), first))
    pieces, orders = gather_pieces(after(tokens, gate_up_own))
    hidden = assemble(pieces, gain[None], bias[None])
    d_pieces, _ = gather_pieces(after(cotangent, *pieces))
    dy = assemble(d_pieces)
    slots = jnp.argsort(block_table[0] % BLK_GROUP).astype(jnp.int32)
    halves = len(orders)
    spots = [(tok ^ apart) * halves + half for apart, half in order_of(orders)]
    place = jnp.argsort(jnp.stack(spots))[slots].astype(jnp.int32)
    tables = rotary_tables()
    d_attended = matmul_nt(dy, out_w).astype(bf16)
    joint_own = split_columns(
        [after(joint_weight, hidden, dy, d_attended, place, *tables)], 3 * own_heads, toks
    )
    joint_own = swap_tok(joint_own).reshape(-1, 3 * span)
    joint_w = gather_grp(after(joint_own, gate_up_w))

    activated, d_gate_up = feed_forward(hidden, dy, gate_up_w, down_w)
    gate_up_term = outer_product(hidden, d_gate_up)
    gate_up_grad = scatter_grp(after(gate_up_term, joint_w))
    down_term = matmul_tn(after(activated, joint_w), dy).astype(bf16)

    joint = matmul(after(hidden, gate_up_term), joint_w)
    attended, d_joint = attention(place, joint, after(d_attended, down_term), tables)
    down_grad = scatter_grp(after(down_term, gate_up_grad, d_joint))
    joint_term = matmul_tn(hidden, d_joint).astype(bf16)
    out_term = matmul_tn(attended, dy).astype(bf16)
    if whole_heads:
        tall = width // grps
        out_term = out_term.reshape(grps, -1, width).reshape(grps * tall, -1)
        joined = jnp.concatenate([joint_term, out_term], axis=1)
        joined = scatter_grp(after(joined, down_grad))
        joint_grad = joined[:, : 3 * span]
        out_grad = joined[:, 3 * span :].reshape(-1, width).astype(f32)
    else:
        joint_grad = scatter_grp(after(joint_term, down_grad))
        spread = jnp.zeros((own_heads, toks, HD, width), bf16)
        spread = lax.dynamic_update_index_in_dim(
            spread, out_term.reshape(own_heads, 1, HD, width), tok, 1
        )
        out_grad = lax.psum_scatter(
            spread.reshape(width, width), both, scatter_dimension=0, tiled=True
        ).astype(f32)
    d_hidden = sum_of_products(
        [after(d_joint, gate_up_grad, joint_term, out_term), d_gate_up], [joint_w, gate_up_w], True
    )
    branch = sum_of_products([after(attended, d_hidden), activated], [out_w, down_w], False)
    d_hidden = scatter_pieces(d_hidden, orders)
    result = (tokens.astype(f32) + scatter_pieces(branch, orders)).astype(bf16)
    tokens_wide = tokens.astype(f32)
    centred = tokens_wide - jnp.mean(tokens_wide, axis=-1, keepdims=True)
    inv_std = lax.rsqrt(jnp.mean(centred * centred, axis=-1, keepdims=True) + eps)
    normed = centred * inv_std
    d_normed = d_hidden * gain
    d_inputs = inv_std * (
        d_normed
        - jnp.mean(d_normed, axis=-1, keepdims=True)
        - normed * jnp.mean(d_normed * normed, axis=-1, keepdims=True)
    )
    input_grad = (cotangent.astype(f32) + d_inputs).astype(bf16)
    sums = jnp.stack([jnp.sum(d_hidden * normed, axis=0), jnp.sum(d_hidden, axis=0)])
    sums = lax.all_to_all(sums.reshape(2, devices, -1).transpose(1, 0, 2), both, 0, 0)
    sums = jnp.sum(sums, axis=0)

    def owned(grad, outer, count):
        return join_columns(swap_tok(grad.reshape(toks, -1, grad.shape[1])), outer, count)

    return (
        result,
        input_grad,
        sums[0],
        sums[1],
        *owned(joint_grad, 3 * own_heads, 1),
        out_grad,
        *owned(gate_up_grad, grps, 2),
        down_grad.astype(f32),
    )


def solution(mesh):
    sharded = P(("grp", "tok"), None)
    vector = P(("grp", "tok"))
    return jax.shard_map(
        body,
        mesh=mesh,
        in_specs=(sharded, sharded, vector, vector) + (sharded,) * 5 + (P("grp", None),),
        out_specs=(sharded, sharded, vector, vector) + (sharded,) * 5,
        check_vma=False,
    )
```

```python
import functools

import jax
import jax.numpy as jnp
from jax import lax
from jax.experimental import pallas as pl
from jax.experimental.pallas import tpu as pltpu
from jax.sharding import PartitionSpec as P

HD = 64
ROT = 16
BT = 128
PB = 8
BLK_GROUP = 16
LANES = 128
QT = 2 * BT

eps = 1e-05
neg_big = -1e30
bf16 = jnp.bfloat16
f32 = jnp.float32
both = ("grp", "tok")
no_cost = pl.CostEstimate(flops=0, transcendentals=0, bytes_accessed=0)


def matmul(left, right):
    return jnp.dot(left, right, preferred_element_type=f32)


def matmul_nt(left, right):
    return lax.dot_general(left, right, (((1,), (1,)), ((), ())), preferred_element_type=f32)


def matmul_tn(left, right):
    return lax.dot_general(left, right, (((0,), (0,)), ((), ())), preferred_element_type=f32)


def rotary_tables():
    positions = (PB + 1) * BT
    freq = 10000.0 ** (-jnp.arange(0, ROT, 2, dtype=f32) / ROT)
    angles = jnp.arange(positions, dtype=jnp.int32).astype(f32)[:, None] * freq[None, :]
    cosine, sine = jnp.cos(angles), jnp.sin(angles)
    rest = jnp.zeros((positions, HD - ROT), f32)
    none = jnp.zeros_like(sine)

    def widen(parts):
        one = jnp.concatenate(parts, axis=1)
        return jnp.concatenate([one] * (LANES // HD), axis=1)

    keep = widen([cosine, cosine, rest + 1.0])
    below = widen([-sine, none, rest])
    above = widen([none, sine, rest])
    return keep, below, above


def attention_kernel(
    place, joint, d_out, keep, below, above, out, d_joint, qs, ks, vs, ds, d_key, d_value
):
    span = d_out.shape[1]
    first = pl.program_id(0) * LANES
    lanes = [pl.ds(pl.multiple_of(c * span + first, LANES), LANES) for c in range(3)]

    def turned(values, part, sign):
        row = min(part, PB) * BT
        c, b, a = (t[row : row + BT, :] for t in (keep, below, above))
        up = pltpu.roll(values, LANES - ROT // 2, 1)
        down = pltpu.roll(values, ROT // 2, 1)
        return values * c + sign * (up * b + down * a)

    def rows_of(part):
        return pl.ds(pl.multiple_of(place[part] * BT, BT), BT)

    for part in range(BLK_GROUP):
        rows = rows_of(part)
        here = pl.ds(part * BT, BT)
        qs[here, :] = turned(joint[rows, lanes[0]], part, 1.0).astype(bf16) * HD ** (-0.5)
        ks[here, :] = turned(joint[rows, lanes[1]], part, 1.0).astype(bf16)
        vs[here, :] = joint[rows, lanes[2]].astype(bf16)
        ds[here, :] = d_out[rows, lanes[0]]

    row_id = lax.broadcasted_iota(jnp.int32, (QT, QT), 0)
    col_id = lax.broadcasted_iota(jnp.int32, (QT, QT), 1)
    causal = row_id >= col_id
    alone = causal & (row_id // BT == col_id // BT)
    head_of = lax.broadcasted_iota(jnp.int32, (QT, LANES), 1) // HD

    def one_head(head, own, shared, allowed):
        mine = head_of == head
        query = jnp.where(mine, qs[own, :], 0).astype(bf16)
        d_o = jnp.where(mine, ds[own, :], 0).astype(bf16)
        spans = [own] + ([pl.ds(0, shared)] if shared else [])
        raw = [matmul_nt(query, ks[s, :]) for s in spans]
        raw[0] = jnp.where(allowed, raw[0], neg_big)
        top = functools.reduce(jnp.maximum, [jnp.max(r, axis=1, keepdims=True) for r in raw])
        terms = [jnp.exp(r - top) for r in raw]
        total = functools.reduce(jnp.add, [jnp.sum(t, axis=1, keepdims=True) for t in terms])
        inverse = 1.0 / total
        weights = [t * inverse for t in terms]
        low = [w.astype(bf16) for w in weights]
        attended = functools.reduce(jnp.add, [matmul(w, vs[s, :]) for w, s in zip(low, spans)])
        delta = jnp.sum(attended * d_o.astype(f32), axis=1, keepdims=True)
        d_scores = [
            (w * (matmul_nt(d_o, vs[s, :]) - delta)).astype(bf16) for w, s in zip(weights, spans)
        ]
        d_query = functools.reduce(jnp.add, [matmul(d, ks[s, :]) for d, s in zip(d_scores, spans)])
        d_keys = [matmul_tn(d, query) for d in d_scores]
        d_values = [matmul_tn(w, d_o) for w in low]
        return attended, d_query, d_keys, d_values

    def tile(index, shared, allowed):
        own = pl.ds(index * QT, QT)
        found = [one_head(head, own, shared, allowed) for head in range(LANES // HD)]
        attended, d_query = found[0][:2]
        for head in range(1, LANES // HD):
            mine = head_of == head
            attended = jnp.where(mine, found[head][0], attended)
            d_query = jnp.where(mine, found[head][1], d_query)
        d_query = d_query * HD ** (-0.5)
        d_keys, d_values = (
            [functools.reduce(jnp.add, parts) for parts in zip(*(f[k] for f in found))]
            for k in (2, 3)
        )
        d_key[own, :] = d_keys[0]
        d_value[own, :] = d_values[0]
        if shared:
            d_key[:shared, :] += d_keys[1]
            d_value[:shared, :] += d_values[1]
        for k in range(QT // BT):
            part = index * (QT // BT) + k
            rows = rows_of(part)
            piece = slice(k * BT, (k + 1) * BT)
            out[rows, lanes[0]] = attended[piece, :].astype(bf16)
            d_joint[rows, lanes[0]] = turned(d_query[piece, :], part, -1.0).astype(bf16)

    prompt_tiles = PB * BT // QT
    for index in range(BLK_GROUP * BT // QT):
        if index < prompt_tiles:
            tile(index, index * QT, causal)
        else:
            tile(index, PB * BT, alone)
    for part in range(BLK_GROUP):
        here = pl.ds(part * BT, BT)
        rows = rows_of(part)
        d_joint[rows, lanes[1]] = turned(d_key[here, :], part, -1.0).astype(bf16)
        d_joint[rows, lanes[2]] = d_value[here, :].astype(bf16)


def attention(place, joint, d_out, tables):
    count, span = d_out.shape
    full = lambda shape: pl.BlockSpec(shape, lambda h, p: (0,) * len(shape))
    scratch = [pltpu.VMEM((count, LANES), bf16)] * 4 + [pltpu.VMEM((count, LANES), f32)] * 2
    return pl.pallas_call(
        attention_kernel,
        grid_spec=pltpu.PrefetchScalarGridSpec(
            num_scalar_prefetch=1,
            grid=(span // LANES,),
            in_specs=[full(joint.shape), full(d_out.shape)] + [full(t.shape) for t in tables],
            out_specs=[full((count, span)), full((count, 3 * span))],
            scratch_shapes=scratch,
        ),
        out_shape=[
            jax.ShapeDtypeStruct((count, span), bf16),
            jax.ShapeDtypeStruct((count, 3 * span), bf16),
        ],
        compiler_params=pltpu.CompilerParams(vmem_limit_bytes=48 * 2**20),
        cost_estimate=no_cost,
    )(place, joint, d_out, *tables)


def after(values, *earlier):
    return lax.optimization_barrier((values, earlier))[0]


def gather_pieces(values, between):
    toks = lax.axis_size("tok")
    bits = toks.bit_length() - 1
    paths = values.shape[0] // BT
    orders = [list(range(1, bits)) + [0], list(range(bits - 1, 0, -1)) + [0]]
    held = list(jnp.split(values, paths))
    found = []
    for step in range(bits):
        if step in between:
            held = between[step](held)
        swaps = [[(i, i ^ (1 << orders[p % 2][step])) for i in range(toks)] for p in range(paths)]
        got = [lax.ppermute(h, "tok", s) for h, s in zip(held, swaps)]
        if step == bits - 1:
            found = [piece for pair in zip(held, got) for piece in pair]
        else:
            held = [jnp.concatenate(pair) for pair in zip(held, got)]
    return found, orders[:paths]


def order_of(orders):
    found = []
    for half, order in enumerate(orders):
        for q in range(1 << len(order)):
            found.append((sum(1 << b for k, b in enumerate(order) if q >> k & 1), half))
    return found


def assemble_kernel(count, norm, *refs):
    pieces, refs = refs[:count], refs[count:]
    step = pl.program_id(0)
    each = pl.num_programs(0) // count
    for k, piece in enumerate(pieces):

        @pl.when(step // each == k)
        def _():
            if norm:
                gain, bias, out = refs
                values = piece[...].astype(f32)
                centred = values - jnp.mean(values, axis=-1, keepdims=True)
                spread = jnp.mean(centred * centred, axis=-1, keepdims=True)
                out[...] = (centred * lax.rsqrt(spread + eps) * gain[...] + bias[...]).astype(bf16)
            else:
                refs[-1][...] = piece[...]


def assemble(pieces, *norm):
    tall, width = pieces[0].shape
    block = min(tall, QT)
    each = tall // block
    total = tall * len(pieces)

    def piece_block(k):
        return pl.BlockSpec((block, width), lambda i: (jnp.clip(i - k * each, 0, each - 1), 0))

    return pl.pallas_call(
        functools.partial(assemble_kernel, len(pieces), bool(norm)),
        grid=(total // block,),
        in_specs=[piece_block(k) for k in range(len(pieces))]
        + [pl.BlockSpec((1, width), lambda i: (0, 0)) for _ in norm],
        out_specs=pl.BlockSpec((block, width), lambda i: (i, 0)),
        out_shape=jax.ShapeDtypeStruct((total, width), bf16),
        compiler_params=pltpu.CompilerParams(vmem_limit_bytes=48 * 2**20),
        cost_estimate=pl.CostEstimate(
            flops=10 * total * width, transcendentals=0, bytes_accessed=8 * total * width
        ),
    )(*pieces, *norm)


def sum_kernel(count, transposed, *refs):
    product = matmul_nt if transposed else matmul
    terms = [product(refs[k][...], refs[count + k][...]) for k in range(count)]
    total = functools.reduce(jnp.add, terms).astype(bf16)
    outs = refs[2 * count :]
    each = pl.num_programs(0) // len(outs)
    for k, out in enumerate(outs):

        @pl.when(pl.program_id(0) // each == k)
        def _():
            out[...] = total


def sum_of_products(lefts, rights, transposed, paths):
    rows = lefts[0].shape[0]
    cols = rights[0].shape[0 if transposed else 1]
    outs = 2 * paths
    each = rows // outs // QT

    def left_block(i):
        which = i // each
        return (which % paths * 2 * each + (1 - which // paths) * each + i % each, 0)

    def out_block(k):
        return pl.BlockSpec((QT, cols), lambda i: (jnp.clip(i - k * each, 0, each - 1), 0))

    found = pl.pallas_call(
        functools.partial(sum_kernel, len(lefts), transposed),
        grid=(rows // QT,),
        in_specs=[pl.BlockSpec((QT, v.shape[1]), left_block) for v in lefts]
        + [pl.BlockSpec(v.shape, lambda i: (0, 0), pipeline_mode=pl.Buffered(1)) for v in rights],
        out_specs=[out_block(k) for k in range(outs)],
        out_shape=[jax.ShapeDtypeStruct((rows // outs, cols), bf16)] * outs,
        compiler_params=pltpu.CompilerParams(vmem_limit_bytes=48 * 2**20),
        cost_estimate=(pl.CostEstimate(flops=18*10**9, transcendentals=0, bytes_accessed=10**7) if transposed else no_cost),
    )(*lefts, *rights)
    return list(zip(found[paths:], found[:paths]))


def feed_kernel(hidden, d_result, up_weight, down_weight, act, d_both):
    wide = act.shape[1]
    both_here = matmul(hidden[...], up_weight[...])
    d_act = matmul_nt(d_result[...], down_weight[...])
    gate, up = both_here[:, :wide], both_here[:, wide:]
    sigma = jax.nn.sigmoid(gate)
    swish = gate * sigma
    act[...] = (swish * up).astype(bf16)
    d_gate = d_act * up * sigma * (1.0 + gate * (1.0 - sigma))
    d_both[...] = jnp.concatenate([d_gate, d_act * swish], axis=1).astype(bf16)


def feed_forward(hidden, d_result, up_weight, down_weight):
    rows, width = hidden.shape
    wide = down_weight.shape[0]
    fixed = lambda w: pl.BlockSpec(w.shape, lambda i: (0, 0), pipeline_mode=pl.Buffered(1))
    return pl.pallas_call(
        feed_kernel,
        grid=(rows // QT,),
        in_specs=[pl.BlockSpec((QT, width), lambda i: (i, 0))] * 2
        + [fixed(up_weight), fixed(down_weight)],
        out_specs=[
            pl.BlockSpec((QT, wide), lambda i: (i, 0)),
            pl.BlockSpec((QT, 2 * wide), lambda i: (i, 0)),
        ],
        out_shape=[
            jax.ShapeDtypeStruct((rows, wide), bf16),
            jax.ShapeDtypeStruct((rows, 2 * wide), bf16),
        ],
        compiler_params=pltpu.CompilerParams(vmem_limit_bytes=48 * 2**20),
        cost_estimate=no_cost,
    )(hidden, d_result, up_weight, down_weight)


def outer_kernel(left, right, out):
    out[...] = matmul_tn(left[...], right[...]).astype(bf16)


def outer_product(left, right):
    rows, tall = left.shape
    wide = right.shape[1]
    return pl.pallas_call(
        outer_kernel,
        grid=(tall // QT,),
        in_specs=[
            pl.BlockSpec((rows, QT), lambda i: (0, i)),
            pl.BlockSpec((rows, wide), lambda i: (0, 0), pipeline_mode=pl.Buffered(1)),
        ],
        out_specs=pl.BlockSpec((QT, wide), lambda i: (i, 0)),
        out_shape=jax.ShapeDtypeStruct((tall, wide), bf16),
        compiler_params=pltpu.CompilerParams(vmem_limit_bytes=48 * 2**20),
        cost_estimate=no_cost,
    )(left, right)


def scatter_step(pairs, orders, step):
    toks = lax.axis_size("tok")
    held = []
    for (kept, sent), order in zip(pairs, orders):
        got = lax.ppermute(sent, "tok", [(i, i ^ (1 << order[step])) for i in range(toks)])
        held.append(kept.astype(f32) + got.astype(f32))
    if not step:
        return held
    tall = held[0].shape[0] // 2
    return lax.optimization_barrier(
        [(h[:tall].astype(bf16), h[tall:].astype(bf16)) for h in held]
    )


def head_terms_kernel(tall, hidden, d_joint, attended, d_result, out):
    grps = pl.num_programs(0) // (tall // QT)
    upper = pl.program_id(0) % grps % (LANES // HD) != 0
    split = d_joint.shape[1]
    out[:, :split] = matmul_tn(hidden[...], d_joint[...]).astype(bf16)
    term = matmul_tn(attended[...], d_result[...])
    term = jnp.where(upper, term[HD:], term[:HD]).astype(bf16)
    wide = out.shape[1] - split
    for k in range(QT // HD):
        out[k * HD : (k + 1) * HD, split:] = term[:, k * wide : (k + 1) * wide]


def head_terms(hidden, d_joint, attended, d_result, grps):
    rows, width = hidden.shape
    tall = width // grps
    each = tall // QT
    wide = HD * width // tall
    return pl.pallas_call(
        functools.partial(head_terms_kernel, tall),
        grid=(each * grps,),
        in_specs=[
            pl.BlockSpec((rows, QT), lambda i: (0, i % grps * each + i // grps)),
            pl.BlockSpec(d_joint.shape, lambda i: (0, 0), pipeline_mode=pl.Buffered(1)),
            pl.BlockSpec((rows, LANES), lambda i: (0, i % grps // (LANES // HD))),
            pl.BlockSpec((rows, width // each), lambda i: (0, i // grps)),
        ],
        out_specs=pl.BlockSpec(
            (QT, d_joint.shape[1] + wide), lambda i: (i % grps * each + i // grps, 0)
        ),
        out_shape=jax.ShapeDtypeStruct((width, d_joint.shape[1] + wide), bf16),
        compiler_params=pltpu.CompilerParams(vmem_limit_bytes=48 * 2**20),
        cost_estimate=no_cost,
    )(hidden, d_joint, attended, d_result)


def gather_grp(values):
    return lax.all_gather(values, "grp", axis=0, tiled=True)


def scatter_grp(values):
    return lax.psum_scatter(values.astype(bf16), "grp", scatter_dimension=0, tiled=True)


def swap_tok(values):
    return lax.all_to_all(values, "tok", 0, 0)


def split_kernel(outer, *refs):
    sources, out = refs[:-1], refs[-1]
    toks = out.shape[0]
    for tok in range(toks):
        pieces = []
        for source in sources:
            inner = source.shape[1] // (outer * toks)
            values = source[...]
            for k in range(outer):
                start = (k * toks + tok) * inner
                pieces.append(values[:, start : start + inner])
        out[tok] = jnp.concatenate(pieces, axis=1)


def split_columns(weights, outer, toks):
    rows = weights[0].shape[0]
    cols = sum(w.shape[1] for w in weights) // toks
    return pl.pallas_call(
        functools.partial(split_kernel, outer),
        out_shape=jax.ShapeDtypeStruct((toks, rows, cols), weights[0].dtype),
        compiler_params=pltpu.CompilerParams(vmem_limit_bytes=32 * 2**20),
    )(*weights)


def join_kernel(outer, source, *outs):
    toks = source.shape[0]
    offset = 0
    for out in outs:
        inner = out.shape[1] // (outer * toks)
        pieces = []
        for k in range(outer):
            for tok in range(toks):
                start = offset + k * inner
                pieces.append(source[tok, :, start : start + inner].astype(f32))
        out[...] = jnp.concatenate(pieces, axis=1)
        offset += outer * inner


def join_columns(parts, outer, count):
    toks, rows, cols = parts.shape
    shape = jax.ShapeDtypeStruct((rows, toks * cols // count), f32)
    return pl.pallas_call(
        functools.partial(join_kernel, outer),
        out_shape=[shape] * count,
        compiler_params=pltpu.CompilerParams(vmem_limit_bytes=32 * 2**20),
    )(parts)


def body(
    tokens,
    cotangent,
    norm_gain,
    norm_bias,
    joint_weight,
    out_weight,
    gate_weight,
    up_weight,
    down_weight,
    block_table,
):
    grps, toks = lax.axis_size("grp"), lax.axis_size("tok")
    devices = grps * toks
    rows, width = tokens.shape
    own_heads = width // HD // toks
    span = own_heads * HD
    wide = gate_weight.shape[1] // toks
    tok = lax.axis_index("tok")

    pair = jnp.stack([norm_gain, norm_bias])
    pair = lax.all_to_all(jnp.broadcast_to(pair[None], (devices,) + pair.shape), both, 0, 0)
    gain = pair[:, 0].reshape(width).astype(f32)
    bias = pair[:, 1].reshape(width).astype(f32)

    tall = width // grps
    whole_heads = out_weight.shape[0] == HD and tall % QT == 0 and HD * grps % LANES == 0
    if whole_heads:
        first = gather_grp(jnp.concatenate([down_weight, out_weight]))
        first = first.reshape(grps, -1, width)
        down_w = first[:, : down_weight.shape[0]].reshape(-1, width)
        out_w = first[:, down_weight.shape[0] :].reshape(-1, width)
    else:
        down_w = first = gather_grp(down_weight)
        out_w = lax.all_gather(out_weight, both, axis=0, tiled=True)
        out_w = lax.dynamic_index_in_dim(
            out_w.reshape(own_heads, toks, HD, width), tok, 1, keepdims=False
        ).reshape(span, width)
    gate_up_own = swap_tok(split_columns([gate_weight, up_weight], grps, toks))
    gate_up_own = gate_up_own.reshape(-1, 2 * wide)
    own_tokens, gate_up_own, gain, bias = lax.optimization_barrier(
        (tokens, gate_up_own, gain, bias)
    )
    tables = rotary_tables()

    def with_tables(held):
        nonlocal tables
        held, tables = lax.optimization_barrier((held, tables))
        return held

    def with_hidden(held):
        nonlocal hidden
        held, hidden = lax.optimization_barrier((held, hidden))
        return held

    pieces, orders = gather_pieces(own_tokens, {2: with_tables})
    own_cotangent, pieces = lax.optimization_barrier((cotangent, pieces))
    hidden = assemble(pieces, gain[None], bias[None])
    slots = jnp.argsort(block_table[0] % BLK_GROUP).astype(jnp.int32)
    halves = len(orders)
    spots = [(tok ^ apart) * halves + half for apart, half in order_of(orders)]
    place = jnp.argsort(jnp.stack(spots))[slots].astype(jnp.int32)
    d_pieces, _ = gather_pieces(own_cotangent, {2: with_hidden})
    gate_up_w = gather_grp(after(gate_up_own, first))
    dy = assemble(d_pieces)
    d_attended = matmul_nt(dy, out_w).astype(bf16)
    joint_own = split_columns(
        [after(joint_weight, dy, d_attended, place)], 3 * own_heads, toks
    )
    joint_own = swap_tok(joint_own).reshape(-1, 3 * span)
    joint_w = gather_grp(after(joint_own, gate_up_w))

    activated, d_gate_up = feed_forward(hidden, dy, gate_up_w, down_w)
    gate_up_term = outer_product(hidden, d_gate_up)
    gate_up_grad = scatter_grp(after(gate_up_term, joint_w))

    joint = matmul(after(hidden, gate_up_term), joint_w)
    attended, d_joint = attention(place, joint, d_attended, tables)
    last = toks.bit_length() - 2
    if whole_heads:
        head_sums = head_terms(hidden, d_joint, attended, dy, grps)
    else:
        head_sums = matmul_tn(hidden, d_joint).astype(bf16)
    flat = lambda pairs: [v for pair in pairs for v in pair]
    lefts = [after(attended, head_sums), activated]
    sums = sum_of_products(lefts, [out_w, down_w], False, halves)
    head_sums = scatter_grp(after(head_sums, gate_up_grad, *flat(sums)))
    sums = scatter_step(sums, orders, last)
    gate_up_rows = swap_tok(after(gate_up_grad, *flat(sums)).reshape(toks, -1, 2 * wide))
    lefts = [after(d_joint, *flat(sums)), d_gate_up]
    d_sums = sum_of_products(lefts, [joint_w, gate_up_w], True, halves)
    sums = scatter_step(sums, orders, last - 1)
    d_sums = scatter_step(d_sums, orders, last)
    d_sums, sums, gate_up_rows = lax.optimization_barrier((d_sums, sums, gate_up_rows))
    down_term = matmul_tn(after(activated, *flat(d_sums)), dy).astype(bf16)
    d_sums = scatter_step(d_sums, orders, last - 1)
    d_sums, sums, head_sums = lax.optimization_barrier((d_sums, sums, head_sums))
    for step in range(last - 2, -1, -1):
        d_sums = scatter_step(d_sums, orders, step)
        sums = scatter_step(sums, orders, step)
    down_grad = scatter_grp(after(down_term, head_sums))
    d_hidden = jnp.concatenate(d_sums)
    result = (tokens.astype(f32) + jnp.concatenate(sums)).astype(bf16)
    if whole_heads:
        joint_grad = head_sums[:, : 3 * span]
        out_grad = head_sums[:, 3 * span :].reshape(tall // HD, HD, -1)
        out_grad = out_grad.transpose(1, 0, 2).reshape(HD, width).astype(f32)
    else:
        joint_grad = head_sums
        spread = jnp.zeros((own_heads, toks, HD, width), bf16)
        out_term = matmul_tn(attended, dy).astype(bf16).reshape(own_heads, 1, HD, width)
        spread = lax.dynamic_update_index_in_dim(spread, out_term, tok, 1)
        out_grad = lax.psum_scatter(
            spread.reshape(width, width), both, scatter_dimension=0, tiled=True
        ).astype(f32)
    tokens_wide = tokens.astype(f32)
    centred = tokens_wide - jnp.mean(tokens_wide, axis=-1, keepdims=True)
    inv_std = lax.rsqrt(jnp.mean(centred * centred, axis=-1, keepdims=True) + eps)
    normed = centred * inv_std
    d_normed = d_hidden * gain
    d_inputs = inv_std * (
        d_normed
        - jnp.mean(d_normed, axis=-1, keepdims=True)
        - normed * jnp.mean(d_normed * normed, axis=-1, keepdims=True)
    )
    input_grad = (cotangent.astype(f32) + d_inputs).astype(bf16)
    sums = jnp.stack([jnp.sum(d_hidden * normed, axis=0), jnp.sum(d_hidden, axis=0)])
    sums = lax.all_to_all(sums.reshape(2, devices, -1).transpose(1, 0, 2), both, 0, 0)
    sums = jnp.sum(sums, axis=0)

    joint_rows = swap_tok(after(joint_grad, d_hidden, result).reshape(toks, -1, 3 * span))

    return (
        result,
        input_grad,
        sums[0],
        sums[1],
        *join_columns(joint_rows, 3 * own_heads, 1),
        out_grad,
        *join_columns(gate_up_rows, grps, 2),
        down_grad.astype(f32),
    )


def solution(mesh):
    sharded = P(("grp", "tok"), None)
    vector = P(("grp", "tok"))
    return jax.shard_map(
        body,
        mesh=mesh,
        in_specs=(sharded, sharded, vector, vector) + (sharded,) * 5 + (P("grp", None),),
        out_specs=(sharded, sharded, vector, vector) + (sharded,) * 5,
        check_vma=False,
    )
```

```python
import functools

import jax
import jax.numpy as jnp
from jax import lax
from jax.experimental import pallas as pl
from jax.experimental.pallas import tpu as pltpu
from jax.sharding import PartitionSpec as P

HD = 64
ROT = 16
BT = 128
PB = 8
BLK_GROUP = 16
LANES = 128
QT = 2 * BT

eps = 1e-05
neg_big = -1e30
bf16 = jnp.bfloat16
f32 = jnp.float32
both = ("grp", "tok")
no_cost = pl.CostEstimate(flops=0, transcendentals=0, bytes_accessed=0)


def matmul(left, right):
    return jnp.dot(left, right, preferred_element_type=f32)


def matmul_nt(left, right):
    return lax.dot_general(left, right, (((1,), (1,)), ((), ())), preferred_element_type=f32)


def matmul_tn(left, right):
    return lax.dot_general(left, right, (((0,), (0,)), ((), ())), preferred_element_type=f32)


def rotary_tables():
    positions = (PB + 1) * BT
    freq = 10000.0 ** (-jnp.arange(0, ROT, 2, dtype=f32) / ROT)
    angles = jnp.arange(positions, dtype=jnp.int32).astype(f32)[:, None] * freq[None, :]
    cosine, sine = jnp.cos(angles), jnp.sin(angles)
    rest = jnp.zeros((positions, HD - ROT), f32)
    none = jnp.zeros_like(sine)

    def widen(parts):
        one = jnp.concatenate(parts, axis=1)
        return jnp.concatenate([one] * (LANES // HD), axis=1)

    keep = widen([cosine, cosine, rest + 1.0])
    below = widen([-sine, none, rest])
    above = widen([none, sine, rest])
    return keep, below, above


def attention_kernel(
    place, joint, d_out, keep, below, above, out, d_joint, qs, ks, vs, ds, d_key, d_value
):
    span = d_out.shape[1]
    first = pl.program_id(0) * LANES
    lanes = [pl.ds(pl.multiple_of(c * span + first, LANES), LANES) for c in range(3)]

    def turned(values, part, sign):
        row = min(part, PB) * BT
        c, b, a = (t[row : row + BT, :] for t in (keep, below, above))
        up = pltpu.roll(values, LANES - ROT // 2, 1)
        down = pltpu.roll(values, ROT // 2, 1)
        return values * c + sign * (up * b + down * a)

    def rows_of(part):
        return pl.ds(pl.multiple_of(place[part] * BT, BT), BT)

    for part in range(BLK_GROUP):
        rows = rows_of(part)
        here = pl.ds(part * BT, BT)
        qs[here, :] = turned(joint[rows, lanes[0]], part, 1.0).astype(bf16) * HD ** (-0.5)
        ks[here, :] = turned(joint[rows, lanes[1]], part, 1.0).astype(bf16)
        vs[here, :] = joint[rows, lanes[2]].astype(bf16)
        ds[here, :] = d_out[rows, lanes[0]]

    row_id = lax.broadcasted_iota(jnp.int32, (QT, QT), 0)
    col_id = lax.broadcasted_iota(jnp.int32, (QT, QT), 1)
    causal = row_id >= col_id
    alone = causal & (row_id // BT == col_id // BT)
    head_of = lax.broadcasted_iota(jnp.int32, (QT, LANES), 1) // HD

    def one_head(head, own, shared, allowed):
        mine = head_of == head
        query = jnp.where(mine, qs[own, :], 0).astype(bf16)
        d_o = jnp.where(mine, ds[own, :], 0).astype(bf16)
        spans = [own] + ([pl.ds(0, shared)] if shared else [])
        raw = [matmul_nt(query, ks[s, :]) for s in spans]
        raw[0] = jnp.where(allowed, raw[0], neg_big)
        top = functools.reduce(jnp.maximum, [jnp.max(r, axis=1, keepdims=True) for r in raw])
        terms = [jnp.exp(r - top) for r in raw]
        total = functools.reduce(jnp.add, [jnp.sum(t, axis=1, keepdims=True) for t in terms])
        inverse = 1.0 / total
        weights = [t * inverse for t in terms]
        low = [w.astype(bf16) for w in weights]
        attended = functools.reduce(jnp.add, [matmul(w, vs[s, :]) for w, s in zip(low, spans)])
        delta = jnp.sum(attended * d_o.astype(f32), axis=1, keepdims=True)
        d_scores = [
            (w * (matmul_nt(d_o, vs[s, :]) - delta)).astype(bf16) for w, s in zip(weights, spans)
        ]
        d_query = functools.reduce(jnp.add, [matmul(d, ks[s, :]) for d, s in zip(d_scores, spans)])
        d_keys = [matmul_tn(d, query) for d in d_scores]
        d_values = [matmul_tn(w, d_o) for w in low]
        return attended, d_query, d_keys, d_values

    def tile(index, shared, allowed):
        own = pl.ds(index * QT, QT)
        found = [one_head(head, own, shared, allowed) for head in range(LANES // HD)]
        attended, d_query = found[0][:2]
        for head in range(1, LANES // HD):
            mine = head_of == head
            attended = jnp.where(mine, found[head][0], attended)
            d_query = jnp.where(mine, found[head][1], d_query)
        d_query = d_query * HD ** (-0.5)
        d_keys, d_values = (
            [functools.reduce(jnp.add, parts) for parts in zip(*(f[k] for f in found))]
            for k in (2, 3)
        )
        d_key[own, :] = d_keys[0]
        d_value[own, :] = d_values[0]
        if shared:
            d_key[:shared, :] += d_keys[1]
            d_value[:shared, :] += d_values[1]
        for k in range(QT // BT):
            part = index * (QT // BT) + k
            rows = rows_of(part)
            piece = slice(k * BT, (k + 1) * BT)
            out[rows, lanes[0]] = attended[piece, :].astype(bf16)
            d_joint[rows, lanes[0]] = turned(d_query[piece, :], part, -1.0).astype(bf16)

    prompt_tiles = PB * BT // QT
    for index in range(BLK_GROUP * BT // QT):
        if index < prompt_tiles:
            tile(index, index * QT, causal)
        else:
            tile(index, PB * BT, alone)
    for part in range(BLK_GROUP):
        here = pl.ds(part * BT, BT)
        rows = rows_of(part)
        d_joint[rows, lanes[1]] = turned(d_key[here, :], part, -1.0).astype(bf16)
        d_joint[rows, lanes[2]] = d_value[here, :].astype(bf16)


def attention(place, joint, d_out, tables):
    count, span = d_out.shape
    full = lambda shape: pl.BlockSpec(shape, lambda h, p: (0,) * len(shape))
    scratch = [pltpu.VMEM((count, LANES), bf16)] * 4 + [pltpu.VMEM((count, LANES), f32)] * 2
    return pl.pallas_call(
        attention_kernel,
        grid_spec=pltpu.PrefetchScalarGridSpec(
            num_scalar_prefetch=1,
            grid=(span // LANES,),
            in_specs=[full(joint.shape), full(d_out.shape)] + [full(t.shape) for t in tables],
            out_specs=[full((count, span)), full((count, 3 * span))],
            scratch_shapes=scratch,
        ),
        out_shape=[
            jax.ShapeDtypeStruct((count, span), bf16),
            jax.ShapeDtypeStruct((count, 3 * span), bf16),
        ],
        compiler_params=pltpu.CompilerParams(vmem_limit_bytes=48 * 2**20),
        cost_estimate=no_cost,
    )(place, joint, d_out, *tables)


def after(values, *earlier):
    return lax.optimization_barrier((values, earlier))[0]


def gather_pieces(values, between):
    toks = lax.axis_size("tok")
    bits = toks.bit_length() - 1
    paths = values.shape[0] // BT
    orders = [list(range(1, bits)) + [0], list(range(bits - 1, 0, -1)) + [0]]
    held = list(jnp.split(values, paths))
    found = []
    for step in range(bits):
        if step in between:
            held = between[step](held)
        swaps = [[(i, i ^ (1 << orders[p % 2][step])) for i in range(toks)] for p in range(paths)]
        got = [lax.ppermute(h, "tok", s) for h, s in zip(held, swaps)]
        if step == bits - 1:
            found = [piece for pair in zip(held, got) for piece in pair]
        else:
            held = [jnp.concatenate(pair) for pair in zip(held, got)]
    return found, orders[:paths]


def order_of(orders):
    found = []
    for half, order in enumerate(orders):
        for q in range(1 << len(order)):
            found.append((sum(1 << b for k, b in enumerate(order) if q >> k & 1), half))
    return found


def assemble_kernel(count, norm, *refs):
    pieces, refs = refs[:count], refs[count:]
    step = pl.program_id(0)
    each = pl.num_programs(0) // count
    for k, piece in enumerate(pieces):

        @pl.when(step // each == k)
        def _():
            if norm:
                gain, bias, out = refs
                values = piece[...].astype(f32)
                centred = values - jnp.mean(values, axis=-1, keepdims=True)
                spread = jnp.mean(centred * centred, axis=-1, keepdims=True)
                out[...] = (centred * lax.rsqrt(spread + eps) * gain[...] + bias[...]).astype(bf16)
            else:
                refs[-1][...] = piece[...]


def assemble(pieces, *norm):
    tall, width = pieces[0].shape
    block = min(tall, QT)
    each = tall // block
    total = tall * len(pieces)

    def piece_block(k):
        return pl.BlockSpec((block, width), lambda i: (jnp.clip(i - k * each, 0, each - 1), 0))

    return pl.pallas_call(
        functools.partial(assemble_kernel, len(pieces), bool(norm)),
        grid=(total // block,),
        in_specs=[piece_block(k) for k in range(len(pieces))]
        + [pl.BlockSpec((1, width), lambda i: (0, 0)) for _ in norm],
        out_specs=pl.BlockSpec((block, width), lambda i: (i, 0)),
        out_shape=jax.ShapeDtypeStruct((total, width), bf16),
        compiler_params=pltpu.CompilerParams(vmem_limit_bytes=48 * 2**20),
        cost_estimate=pl.CostEstimate(
            flops=10 * total * width, transcendentals=0, bytes_accessed=8 * total * width
        ),
    )(*pieces, *norm)


def sum_kernel(count, transposed, *refs):
    product = matmul_nt if transposed else matmul
    terms = [product(refs[k][...], refs[count + k][...]) for k in range(count)]
    total = functools.reduce(jnp.add, terms).astype(bf16)
    outs = refs[2 * count :]
    each = pl.num_programs(0) // len(outs)
    for k, out in enumerate(outs):

        @pl.when(pl.program_id(0) // each == k)
        def _():
            out[...] = total


def sum_of_products(lefts, rights, transposed, paths):
    rows = lefts[0].shape[0]
    cols = rights[0].shape[0 if transposed else 1]
    outs = 2 * paths
    each = rows // outs // QT

    def left_block(i):
        which = i // each
        return (which % paths * 2 * each + (1 - which // paths) * each + i % each, 0)

    def out_block(k):
        return pl.BlockSpec((QT, cols), lambda i: (jnp.clip(i - k * each, 0, each - 1), 0))

    found = pl.pallas_call(
        functools.partial(sum_kernel, len(lefts), transposed),
        grid=(rows // QT,),
        in_specs=[pl.BlockSpec((QT, v.shape[1]), left_block) for v in lefts]
        + [pl.BlockSpec(v.shape, lambda i: (0, 0), pipeline_mode=pl.Buffered(1)) for v in rights],
        out_specs=[out_block(k) for k in range(outs)],
        out_shape=[jax.ShapeDtypeStruct((rows // outs, cols), bf16)] * outs,
        compiler_params=pltpu.CompilerParams(vmem_limit_bytes=48 * 2**20),
        cost_estimate=(pl.CostEstimate(flops=18*10**9, transcendentals=0, bytes_accessed=10**7) if transposed else no_cost),
    )(*lefts, *rights)
    return list(zip(found[paths:], found[:paths]))


def feed_kernel(hidden, d_result, up_weight, down_weight, act, d_both):
    wide = act.shape[1]
    both_here = matmul(hidden[...], up_weight[...])
    d_act = matmul_nt(d_result[...], down_weight[...])
    gate, up = both_here[:, :wide], both_here[:, wide:]
    sigma = jax.nn.sigmoid(gate)
    swish = gate * sigma
    act[...] = (swish * up).astype(bf16)
    d_gate = d_act * up * sigma * (1.0 + gate * (1.0 - sigma))
    d_both[...] = jnp.concatenate([d_gate, d_act * swish], axis=1).astype(bf16)


def feed_forward(hidden, d_result, up_weight, down_weight):
    rows, width = hidden.shape
    wide = down_weight.shape[0]
    fixed = lambda w: pl.BlockSpec(w.shape, lambda i: (0, 0), pipeline_mode=pl.Buffered(1))
    return pl.pallas_call(
        feed_kernel,
        grid=(rows // QT,),
        in_specs=[pl.BlockSpec((QT, width), lambda i: (i, 0))] * 2
        + [fixed(up_weight), fixed(down_weight)],
        out_specs=[
            pl.BlockSpec((QT, wide), lambda i: (i, 0)),
            pl.BlockSpec((QT, 2 * wide), lambda i: (i, 0)),
        ],
        out_shape=[
            jax.ShapeDtypeStruct((rows, wide), bf16),
            jax.ShapeDtypeStruct((rows, 2 * wide), bf16),
        ],
        compiler_params=pltpu.CompilerParams(vmem_limit_bytes=48 * 2**20),
        cost_estimate=no_cost,
    )(hidden, d_result, up_weight, down_weight)


def outer_kernel(left, right, out):
    out[...] = matmul_tn(left[...], right[...]).astype(bf16)


def outer_product(left, right):
    rows, tall = left.shape
    wide = right.shape[1]
    return pl.pallas_call(
        outer_kernel,
        grid=(tall // QT,),
        in_specs=[
            pl.BlockSpec((rows, QT), lambda i: (0, i)),
            pl.BlockSpec((rows, wide), lambda i: (0, 0), pipeline_mode=pl.Buffered(1)),
        ],
        out_specs=pl.BlockSpec((QT, wide), lambda i: (i, 0)),
        out_shape=jax.ShapeDtypeStruct((tall, wide), bf16),
        compiler_params=pltpu.CompilerParams(vmem_limit_bytes=48 * 2**20),
        cost_estimate=no_cost,
    )(left, right)


def scatter_step(pairs, orders, step):
    toks = lax.axis_size("tok")
    held = []
    for (kept, sent), order in zip(pairs, orders):
        got = lax.ppermute(sent, "tok", [(i, i ^ (1 << order[step])) for i in range(toks)])
        held.append(kept.astype(f32) + got.astype(f32))
    if not step:
        return held
    tall = held[0].shape[0] // 2
    return lax.optimization_barrier(
        [(h[:tall].astype(bf16), h[tall:].astype(bf16)) for h in held]
    )


def head_terms_kernel(tall, hidden, d_joint, attended, d_result, out):
    grps = pl.num_programs(0) // (tall // QT)
    upper = pl.program_id(0) % grps % (LANES // HD) != 0
    split = d_joint.shape[1]
    out[:, :split] = matmul_tn(hidden[...], d_joint[...]).astype(bf16)
    term = matmul_tn(attended[...], d_result[...])
    term = jnp.where(upper, term[HD:], term[:HD]).astype(bf16)
    wide = out.shape[1] - split
    for k in range(QT // HD):
        out[k * HD : (k + 1) * HD, split:] = term[:, k * wide : (k + 1) * wide]


def head_terms(hidden, d_joint, attended, d_result, grps):
    rows, width = hidden.shape
    tall = width // grps
    each = tall // QT
    wide = HD * width // tall
    return pl.pallas_call(
        functools.partial(head_terms_kernel, tall),
        grid=(each * grps,),
        in_specs=[
            pl.BlockSpec((rows, QT), lambda i: (0, i % grps * each + i // grps)),
            pl.BlockSpec(d_joint.shape, lambda i: (0, 0), pipeline_mode=pl.Buffered(1)),
            pl.BlockSpec((rows, LANES), lambda i: (0, i % grps // (LANES // HD))),
            pl.BlockSpec((rows, width // each), lambda i: (0, i // grps)),
        ],
        out_specs=pl.BlockSpec(
            (QT, d_joint.shape[1] + wide), lambda i: (i % grps * each + i // grps, 0)
        ),
        out_shape=jax.ShapeDtypeStruct((width, d_joint.shape[1] + wide), bf16),
        compiler_params=pltpu.CompilerParams(vmem_limit_bytes=48 * 2**20),
        cost_estimate=no_cost,
    )(hidden, d_joint, attended, d_result)


def gather_grp(values):
    return lax.all_gather(values, "grp", axis=0, tiled=True)


def scatter_grp(values):
    return lax.psum_scatter(values.astype(bf16), "grp", scatter_dimension=0, tiled=True)


def swap_tok(values):
    return lax.all_to_all(values, "tok", 0, 0)


def split_kernel(outer, *refs):
    sources, out = refs[:-1], refs[-1]
    toks = out.shape[0]
    for tok in range(toks):
        pieces = []
        for source in sources:
            inner = source.shape[1] // (outer * toks)
            values = source[...]
            for k in range(outer):
                start = (k * toks + tok) * inner
                pieces.append(values[:, start : start + inner])
        out[tok] = jnp.concatenate(pieces, axis=1)


def split_columns(weights, outer, toks):
    rows = weights[0].shape[0]
    cols = sum(w.shape[1] for w in weights) // toks
    return pl.pallas_call(
        functools.partial(split_kernel, outer),
        out_shape=jax.ShapeDtypeStruct((toks, rows, cols), weights[0].dtype),
        compiler_params=pltpu.CompilerParams(vmem_limit_bytes=32 * 2**20),
    )(*weights)


def join_kernel(outer, source, *outs):
    toks = source.shape[0]
    offset = 0
    for out in outs:
        inner = out.shape[1] // (outer * toks)
        pieces = []
        for k in range(outer):
            for tok in range(toks):
                start = offset + k * inner
                pieces.append(source[tok, :, start : start + inner].astype(f32))
        out[...] = jnp.concatenate(pieces, axis=1)
        offset += outer * inner


def join_columns(parts, outer, count):
    toks, rows, cols = parts.shape
    shape = jax.ShapeDtypeStruct((rows, toks * cols // count), f32)
    return pl.pallas_call(
        functools.partial(join_kernel, outer),
        out_shape=[shape] * count,
        compiler_params=pltpu.CompilerParams(vmem_limit_bytes=32 * 2**20),
    )(parts)


def body(
    tokens,
    cotangent,
    norm_gain,
    norm_bias,
    joint_weight,
    out_weight,
    gate_weight,
    up_weight,
    down_weight,
    block_table,
):
    grps, toks = lax.axis_size("grp"), lax.axis_size("tok")
    devices = grps * toks
    rows, width = tokens.shape
    own_heads = width // HD // toks
    span = own_heads * HD
    wide = gate_weight.shape[1] // toks
    tok = lax.axis_index("tok")

    pair = jnp.stack([norm_gain, norm_bias])
    pair = lax.all_to_all(jnp.broadcast_to(pair[None], (devices,) + pair.shape), both, 0, 0)
    gain = pair[:, 0].reshape(width).astype(f32)
    bias = pair[:, 1].reshape(width).astype(f32)

    tall = width // grps
    whole_heads = out_weight.shape[0] == HD and tall % QT == 0 and HD * grps % LANES == 0
    if whole_heads:
        first = gather_grp(jnp.concatenate([down_weight, out_weight]))
        first = first.reshape(grps, -1, width)
        down_w = first[:, : down_weight.shape[0]].reshape(-1, width)
        out_w = first[:, down_weight.shape[0] :].reshape(-1, width)
    else:
        down_w = first = gather_grp(down_weight)
        out_w = lax.all_gather(out_weight, both, axis=0, tiled=True)
        out_w = lax.dynamic_index_in_dim(
            out_w.reshape(own_heads, toks, HD, width), tok, 1, keepdims=False
        ).reshape(span, width)
    gate_up_own = swap_tok(split_columns([gate_weight, up_weight], grps, toks))
    gate_up_own = gate_up_own.reshape(-1, 2 * wide)
    own_tokens, gate_up_own, gain, bias = lax.optimization_barrier(
        (tokens, gate_up_own, gain, bias)
    )
    tables = rotary_tables()

    def with_tables(held):
        nonlocal tables
        held, tables = lax.optimization_barrier((held, tables))
        return held

    def with_hidden(held):
        nonlocal hidden
        held, hidden = lax.optimization_barrier((held, hidden))
        return held

    pieces, orders = gather_pieces(own_tokens, {2: with_tables})
    own_cotangent, pieces = lax.optimization_barrier((cotangent, pieces))
    hidden = assemble(pieces, gain[None], bias[None])
    slots = jnp.argsort(block_table[0] % BLK_GROUP).astype(jnp.int32)
    halves = len(orders)
    spots = [(tok ^ apart) * halves + half for apart, half in order_of(orders)]
    place = jnp.argsort(jnp.stack(spots))[slots].astype(jnp.int32)
    d_pieces, _ = gather_pieces(own_cotangent, {2: with_hidden})
    gate_up_w = gather_grp(after(gate_up_own, first))
    dy = assemble(d_pieces)
    d_attended = matmul_nt(dy, out_w).astype(bf16)
    joint_own = split_columns(
        [after(joint_weight, dy, d_attended, place)], 3 * own_heads, toks
    )
    joint_own = swap_tok(joint_own).reshape(-1, 3 * span)
    joint_w = gather_grp(after(joint_own, gate_up_w))

    activated, d_gate_up = feed_forward(hidden, dy, gate_up_w, down_w)
    gate_up_term = outer_product(hidden, d_gate_up)
    gate_up_grad = scatter_grp(after(gate_up_term, joint_w))

    joint = matmul(after(hidden, gate_up_term), joint_w)
    attended, d_joint = attention(place, joint, d_attended, tables)
    last = toks.bit_length() - 2
    if whole_heads:
        head_sums = head_terms(hidden, d_joint, attended, dy, grps)
    else:
        head_sums = matmul_tn(hidden, d_joint).astype(bf16)
    flat = lambda pairs: [v for pair in pairs for v in pair]
    lefts = [after(attended, head_sums), activated]
    sums = sum_of_products(lefts, [out_w, down_w], False, halves)
    head_sums = scatter_grp(after(head_sums, gate_up_grad))
    sums = scatter_step(sums, orders, last)
    gate_up_rows = swap_tok(after(gate_up_grad, *flat(sums)).reshape(toks, -1, 2 * wide))
    lefts = [after(d_joint, *flat(sums)), d_gate_up]
    d_sums = sum_of_products(lefts, [joint_w, gate_up_w], True, halves)
    d_sums, gate_up_rows = lax.optimization_barrier((d_sums, gate_up_rows))
    sums = scatter_step(sums, orders, last - 1)
    d_sums = scatter_step(d_sums, orders, last)
    d_sums, sums = lax.optimization_barrier((d_sums, sums))
    down_term = matmul_tn(after(activated, *flat(d_sums)), dy).astype(bf16)
    for step in range(last - 2, -1, -1):
        sums = scatter_step(sums, orders, step)
    kept, head_sums = lax.optimization_barrier(([pair[0] for pair in d_sums], head_sums))
    d_sums = [(k, pair[1]) for k, pair in zip(kept, d_sums)]
    d_sums = scatter_step(d_sums, orders, last - 1)
    sums, d_sums = lax.optimization_barrier((sums, d_sums))
    head_rows = after(head_sums[:, : 3 * span], *flat(d_sums))
    head_rows = swap_tok(head_rows.reshape(toks, -1, 3 * span))
    kept, head_rows = lax.optimization_barrier(([pair[0] for pair in d_sums], head_rows))
    d_sums = [(k, pair[1]) for k, pair in zip(kept, d_sums)]
    for step in range(last - 2, -1, -1):
        d_sums = scatter_step(d_sums, orders, step)
    down_grad = scatter_grp(after(down_term, head_sums))
    d_hidden = jnp.concatenate(d_sums)
    result = (tokens.astype(f32) + jnp.concatenate(sums)).astype(bf16)
    if whole_heads:
        out_grad = head_sums[:, 3 * span :].reshape(tall // HD, HD, -1)
        out_grad = out_grad.transpose(1, 0, 2).reshape(HD, width).astype(f32)
    else:
        spread = jnp.zeros((own_heads, toks, HD, width), bf16)
        out_term = matmul_tn(attended, dy).astype(bf16).reshape(own_heads, 1, HD, width)
        spread = lax.dynamic_update_index_in_dim(spread, out_term, tok, 1)
        out_grad = lax.psum_scatter(
            spread.reshape(width, width), both, scatter_dimension=0, tiled=True
        ).astype(f32)
    tokens_wide = tokens.astype(f32)
    centred = tokens_wide - jnp.mean(tokens_wide, axis=-1, keepdims=True)
    inv_std = lax.rsqrt(jnp.mean(centred * centred, axis=-1, keepdims=True) + eps)
    normed = centred * inv_std
    d_normed = d_hidden * gain
    d_inputs = inv_std * (
        d_normed
        - jnp.mean(d_normed, axis=-1, keepdims=True)
        - normed * jnp.mean(d_normed * normed, axis=-1, keepdims=True)
    )
    input_grad = (cotangent.astype(f32) + d_inputs).astype(bf16)
    sums = jnp.stack([jnp.sum(d_hidden * normed, axis=0), jnp.sum(d_hidden, axis=0)])
    sums = lax.all_to_all(sums.reshape(2, devices, -1).transpose(1, 0, 2), both, 0, 0)
    sums = jnp.sum(sums, axis=0)

    return (
        result,
        input_grad,
        sums[0],
        sums[1],
        *join_columns(head_rows, 3 * own_heads, 1),
        out_grad,
        *join_columns(gate_up_rows, grps, 2),
        down_grad.astype(f32),
    )


def solution(mesh):
    sharded = P(("grp", "tok"), None)
    vector = P(("grp", "tok"))
    return jax.shard_map(
        body,
        mesh=mesh,
        in_specs=(sharded, sharded, vector, vector) + (sharded,) * 5 + (P("grp", None),),
        out_specs=(sharded, sharded, vector, vector) + (sharded,) * 5,
        check_vma=False,
    )
```

```python
import functools

import jax
import jax.numpy as jnp
from jax import lax
from jax.experimental import pallas as pl
from jax.experimental.pallas import tpu as pltpu
from jax.sharding import PartitionSpec as P

HD = 64
ROT = 16
BT = 128
PB = 8
BLK_GROUP = 16
LANES = 128
QT = 2 * BT

eps = 1e-05
neg_big = -1e30
bf16 = jnp.bfloat16
f32 = jnp.float32
both = ("grp", "tok")
no_cost = pl.CostEstimate(flops=0, transcendentals=0, bytes_accessed=0)


def matmul(left, right):
    return jnp.dot(left, right, preferred_element_type=f32)


def matmul_nt(left, right):
    return lax.dot_general(left, right, (((1,), (1,)), ((), ())), preferred_element_type=f32)


def matmul_tn(left, right):
    return lax.dot_general(left, right, (((0,), (0,)), ((), ())), preferred_element_type=f32)


def rotary_tables():
    positions = (PB + 1) * BT
    freq = 10000.0 ** (-jnp.arange(0, ROT, 2, dtype=f32) / ROT)
    angles = jnp.arange(positions, dtype=jnp.int32).astype(f32)[:, None] * freq[None, :]
    cosine, sine = jnp.cos(angles), jnp.sin(angles)
    rest = jnp.zeros((positions, HD - ROT), f32)
    none = jnp.zeros_like(sine)

    def widen(parts):
        one = jnp.concatenate(parts, axis=1)
        return jnp.concatenate([one] * (LANES // HD), axis=1)

    keep = widen([cosine, cosine, rest + 1.0])
    below = widen([-sine, none, rest])
    above = widen([none, sine, rest])
    return keep, below, above


def attention_kernel(
    place, joint, d_out, keep, below, above, out, d_joint, qs, ks, vs, ds, d_key, d_value
):
    span = d_out.shape[1]
    first = pl.program_id(0) * LANES
    lanes = [pl.ds(pl.multiple_of(c * span + first, LANES), LANES) for c in range(3)]

    def turned(values, part, sign):
        row = min(part, PB) * BT
        c, b, a = (t[row : row + BT, :] for t in (keep, below, above))
        up = pltpu.roll(values, LANES - ROT // 2, 1)
        down = pltpu.roll(values, ROT // 2, 1)
        return values * c + sign * (up * b + down * a)

    def rows_of(part):
        return pl.ds(pl.multiple_of(place[part] * BT, BT), BT)

    for part in range(BLK_GROUP):
        rows = rows_of(part)
        here = pl.ds(part * BT, BT)
        qs[here, :] = turned(joint[rows, lanes[0]], part, 1.0).astype(bf16) * HD ** (-0.5)
        ks[here, :] = turned(joint[rows, lanes[1]], part, 1.0).astype(bf16)
        vs[here, :] = joint[rows, lanes[2]].astype(bf16)
        ds[here, :] = d_out[rows, lanes[0]]

    row_id = lax.broadcasted_iota(jnp.int32, (QT, QT), 0)
    col_id = lax.broadcasted_iota(jnp.int32, (QT, QT), 1)
    causal = row_id >= col_id
    alone = causal & (row_id // BT == col_id // BT)
    head_of = lax.broadcasted_iota(jnp.int32, (QT, LANES), 1) // HD

    def one_head(head, own, shared, allowed):
        mine = head_of == head
        query = jnp.where(mine, qs[own, :], 0).astype(bf16)
        d_o = jnp.where(mine, ds[own, :], 0).astype(bf16)
        spans = [own] + ([pl.ds(0, shared)] if shared else [])
        raw = [matmul_nt(query, ks[s, :]) for s in spans]
        raw[0] = jnp.where(allowed, raw[0], neg_big)
        top = functools.reduce(jnp.maximum, [jnp.max(r, axis=1, keepdims=True) for r in raw])
        terms = [jnp.exp(r - top) for r in raw]
        total = functools.reduce(jnp.add, [jnp.sum(t, axis=1, keepdims=True) for t in terms])
        inverse = 1.0 / total
        weights = [t * inverse for t in terms]
        low = [w.astype(bf16) for w in weights]
        attended = functools.reduce(jnp.add, [matmul(w, vs[s, :]) for w, s in zip(low, spans)])
        delta = jnp.sum(attended * d_o.astype(f32), axis=1, keepdims=True)
        d_scores = [
            (w * (matmul_nt(d_o, vs[s, :]) - delta)).astype(bf16) for w, s in zip(weights, spans)
        ]
        d_query = functools.reduce(jnp.add, [matmul(d, ks[s, :]) for d, s in zip(d_scores, spans)])
        d_keys = [matmul_tn(d, query) for d in d_scores]
        d_values = [matmul_tn(w, d_o) for w in low]
        return attended, d_query, d_keys, d_values

    def tile(index, shared, allowed):
        own = pl.ds(index * QT, QT)
        found = [one_head(head, own, shared, allowed) for head in range(LANES // HD)]
        attended, d_query = found[0][:2]
        for head in range(1, LANES // HD):
            mine = head_of == head
            attended = jnp.where(mine, found[head][0], attended)
            d_query = jnp.where(mine, found[head][1], d_query)
        d_query = d_query * HD ** (-0.5)
        d_keys, d_values = (
            [functools.reduce(jnp.add, parts) for parts in zip(*(f[k] for f in found))]
            for k in (2, 3)
        )
        d_key[own, :] = d_keys[0]
        d_value[own, :] = d_values[0]
        if shared:
            d_key[:shared, :] += d_keys[1]
            d_value[:shared, :] += d_values[1]
        for k in range(QT // BT):
            part = index * (QT // BT) + k
            rows = rows_of(part)
            piece = slice(k * BT, (k + 1) * BT)
            out[rows, lanes[0]] = attended[piece, :].astype(bf16)
            d_joint[rows, lanes[0]] = turned(d_query[piece, :], part, -1.0).astype(bf16)

    prompt_tiles = PB * BT // QT
    for index in range(BLK_GROUP * BT // QT):
        if index < prompt_tiles:
            tile(index, index * QT, causal)
        else:
            tile(index, PB * BT, alone)
    for part in range(BLK_GROUP):
        here = pl.ds(part * BT, BT)
        rows = rows_of(part)
        d_joint[rows, lanes[1]] = turned(d_key[here, :], part, -1.0).astype(bf16)
        d_joint[rows, lanes[2]] = d_value[here, :].astype(bf16)


def attention(place, joint, d_out, tables):
    count, span = d_out.shape
    full = lambda shape: pl.BlockSpec(shape, lambda h, p: (0,) * len(shape))
    scratch = [pltpu.VMEM((count, LANES), bf16)] * 4 + [pltpu.VMEM((count, LANES), f32)] * 2
    return pl.pallas_call(
        attention_kernel,
        grid_spec=pltpu.PrefetchScalarGridSpec(
            num_scalar_prefetch=1,
            grid=(span // LANES,),
            in_specs=[full(joint.shape), full(d_out.shape)] + [full(t.shape) for t in tables],
            out_specs=[full((count, span)), full((count, 3 * span))],
            scratch_shapes=scratch,
        ),
        out_shape=[
            jax.ShapeDtypeStruct((count, span), bf16),
            jax.ShapeDtypeStruct((count, 3 * span), bf16),
        ],
        compiler_params=pltpu.CompilerParams(vmem_limit_bytes=48 * 2**20),
        cost_estimate=no_cost,
    )(place, joint, d_out, *tables)


def after(values, *earlier):
    return lax.optimization_barrier((values, earlier))[0]


def gather_pieces(values, between):
    toks = lax.axis_size("tok")
    bits = toks.bit_length() - 1
    paths = values.shape[0] // BT
    orders = [list(range(1, bits)) + [0], list(range(bits - 1, 0, -1)) + [0]]
    held = list(jnp.split(values, paths))
    found = []
    for step in range(bits):
        if step in between:
            held = between[step](held)
        swaps = [[(i, i ^ (1 << orders[p % 2][step])) for i in range(toks)] for p in range(paths)]
        got = [lax.ppermute(h, "tok", s) for h, s in zip(held, swaps)]
        if step == bits - 1:
            found = [piece for pair in zip(held, got) for piece in pair]
        else:
            held = [jnp.concatenate(pair) for pair in zip(held, got)]
    return found, orders[:paths]


def order_of(orders):
    found = []
    for half, order in enumerate(orders):
        for q in range(1 << len(order)):
            found.append((sum(1 << b for k, b in enumerate(order) if q >> k & 1), half))
    return found


def assemble_kernel(count, norm, *refs):
    pieces, refs = refs[:count], refs[count:]
    step = pl.program_id(0)
    each = pl.num_programs(0) // count
    for k, piece in enumerate(pieces):

        @pl.when(step // each == k)
        def _():
            if norm:
                gain, bias, out = refs
                values = piece[...].astype(f32)
                centred = values - jnp.mean(values, axis=-1, keepdims=True)
                spread = jnp.mean(centred * centred, axis=-1, keepdims=True)
                out[...] = (centred * lax.rsqrt(spread + eps) * gain[...] + bias[...]).astype(bf16)
            else:
                refs[-1][...] = piece[...]


def assemble(pieces, *norm):
    tall, width = pieces[0].shape
    block = min(tall, QT)
    each = tall // block
    total = tall * len(pieces)

    def piece_block(k):
        return pl.BlockSpec((block, width), lambda i: (jnp.clip(i - k * each, 0, each - 1), 0))

    return pl.pallas_call(
        functools.partial(assemble_kernel, len(pieces), bool(norm)),
        grid=(total // block,),
        in_specs=[piece_block(k) for k in range(len(pieces))]
        + [pl.BlockSpec((1, width), lambda i: (0, 0)) for _ in norm],
        out_specs=pl.BlockSpec((block, width), lambda i: (i, 0)),
        out_shape=jax.ShapeDtypeStruct((total, width), bf16),
        compiler_params=pltpu.CompilerParams(vmem_limit_bytes=48 * 2**20),
        cost_estimate=pl.CostEstimate(
            flops=10 * total * width, transcendentals=0, bytes_accessed=8 * total * width
        ),
    )(*pieces, *norm)


def sum_kernel(count, transposed, *refs):
    product = matmul_nt if transposed else matmul
    terms = [product(refs[k][...], refs[count + k][...]) for k in range(count)]
    total = functools.reduce(jnp.add, terms).astype(bf16)
    outs = refs[2 * count :]
    each = pl.num_programs(0) // len(outs)
    for k, out in enumerate(outs):

        @pl.when(pl.program_id(0) // each == k)
        def _():
            out[...] = total


def sum_of_products(lefts, rights, transposed, paths):
    rows = lefts[0].shape[0]
    cols = rights[0].shape[0 if transposed else 1]
    outs = 2 * paths
    each = rows // outs // QT

    def left_block(i):
        which = i // each
        return (which % paths * 2 * each + (1 - which // paths) * each + i % each, 0)

    def out_block(k):
        return pl.BlockSpec((QT, cols), lambda i: (jnp.clip(i - k * each, 0, each - 1), 0))

    found = pl.pallas_call(
        functools.partial(sum_kernel, len(lefts), transposed),
        grid=(rows // QT,),
        in_specs=[pl.BlockSpec((QT, v.shape[1]), left_block) for v in lefts]
        + [pl.BlockSpec(v.shape, lambda i: (0, 0), pipeline_mode=pl.Buffered(1)) for v in rights],
        out_specs=[out_block(k) for k in range(outs)],
        out_shape=[jax.ShapeDtypeStruct((rows // outs, cols), bf16)] * outs,
        compiler_params=pltpu.CompilerParams(vmem_limit_bytes=48 * 2**20),
        cost_estimate=no_cost,
    )(*lefts, *rights)
    return list(zip(found[paths:], found[:paths]))


def feed_kernel(hidden, d_result, up_weight, down_weight, act, d_both):
    wide = act.shape[1]
    both_here = matmul(hidden[...], up_weight[...])
    d_act = matmul_nt(d_result[...], down_weight[...])
    gate, up = both_here[:, :wide], both_here[:, wide:]
    sigma = jax.nn.sigmoid(gate)
    swish = gate * sigma
    act[...] = (swish * up).astype(bf16)
    d_gate = d_act * up * sigma * (1.0 + gate * (1.0 - sigma))
    d_both[...] = jnp.concatenate([d_gate, d_act * swish], axis=1).astype(bf16)


def feed_forward(hidden, d_result, up_weight, down_weight):
    rows, width = hidden.shape
    wide = down_weight.shape[0]
    fixed = lambda w: pl.BlockSpec(w.shape, lambda i: (0, 0), pipeline_mode=pl.Buffered(1))
    return pl.pallas_call(
        feed_kernel,
        grid=(rows // QT,),
        in_specs=[pl.BlockSpec((QT, width), lambda i: (i, 0))] * 2
        + [fixed(up_weight), fixed(down_weight)],
        out_specs=[
            pl.BlockSpec((QT, wide), lambda i: (i, 0)),
            pl.BlockSpec((QT, 2 * wide), lambda i: (i, 0)),
        ],
        out_shape=[
            jax.ShapeDtypeStruct((rows, wide), bf16),
            jax.ShapeDtypeStruct((rows, 2 * wide), bf16),
        ],
        compiler_params=pltpu.CompilerParams(vmem_limit_bytes=48 * 2**20),
        cost_estimate=no_cost,
    )(hidden, d_result, up_weight, down_weight)


def outer_kernel(left, right, out):
    out[...] = matmul_tn(left[...], right[...]).astype(bf16)


def outer_product(left, right):
    rows, tall = left.shape
    wide = right.shape[1]
    return pl.pallas_call(
        outer_kernel,
        grid=(tall // QT,),
        in_specs=[
            pl.BlockSpec((rows, QT), lambda i: (0, i)),
            pl.BlockSpec((rows, wide), lambda i: (0, 0), pipeline_mode=pl.Buffered(1)),
        ],
        out_specs=pl.BlockSpec((QT, wide), lambda i: (i, 0)),
        out_shape=jax.ShapeDtypeStruct((tall, wide), bf16),
        compiler_params=pltpu.CompilerParams(vmem_limit_bytes=48 * 2**20),
        cost_estimate=no_cost,
    )(left, right)


def scatter_step(pairs, orders, step):
    toks = lax.axis_size("tok")
    held = []
    for (kept, sent), order in zip(pairs, orders):
        got = lax.ppermute(sent, "tok", [(i, i ^ (1 << order[step])) for i in range(toks)])
        held.append(kept.astype(f32) + got.astype(f32))
    if not step:
        return held
    tall = held[0].shape[0] // 2
    return lax.optimization_barrier(
        [(h[:tall].astype(bf16), h[tall:].astype(bf16)) for h in held]
    )


def head_terms_kernel(tall, hidden, d_joint, attended, d_result, out):
    grps = pl.num_programs(0) // (tall // QT)
    upper = pl.program_id(0) % grps % (LANES // HD) != 0
    split = d_joint.shape[1]
    out[:, :split] = matmul_tn(hidden[...], d_joint[...]).astype(bf16)
    term = matmul_tn(attended[...], d_result[...])
    term = jnp.where(upper, term[HD:], term[:HD]).astype(bf16)
    wide = out.shape[1] - split
    for k in range(QT // HD):
        out[k * HD : (k + 1) * HD, split:] = term[:, k * wide : (k + 1) * wide]


def head_terms(hidden, d_joint, attended, d_result, grps):
    rows, width = hidden.shape
    tall = width // grps
    each = tall // QT
    wide = HD * width // tall
    return pl.pallas_call(
        functools.partial(head_terms_kernel, tall),
        grid=(each * grps,),
        in_specs=[
            pl.BlockSpec((rows, QT), lambda i: (0, i % grps * each + i // grps)),
            pl.BlockSpec(d_joint.shape, lambda i: (0, 0), pipeline_mode=pl.Buffered(1)),
            pl.BlockSpec((rows, LANES), lambda i: (0, i % grps // (LANES // HD))),
            pl.BlockSpec((rows, width // each), lambda i: (0, i // grps)),
        ],
        out_specs=pl.BlockSpec(
            (QT, d_joint.shape[1] + wide), lambda i: (i % grps * each + i // grps, 0)
        ),
        out_shape=jax.ShapeDtypeStruct((width, d_joint.shape[1] + wide), bf16),
        compiler_params=pltpu.CompilerParams(vmem_limit_bytes=48 * 2**20),
        cost_estimate=pl.CostEstimate(
            flops=10**10, transcendentals=0, bytes_accessed=10**7
        ),
    )(hidden, d_joint, attended, d_result)


def gather_grp(values):
    return lax.all_gather(values, "grp", axis=0, tiled=True)


def scatter_grp(values):
    return lax.psum_scatter(values.astype(bf16), "grp", scatter_dimension=0, tiled=True)


def swap_tok(values):
    return lax.all_to_all(values, "tok", 0, 0)


def split_kernel(outer, *refs):
    sources, out = refs[:-1], refs[-1]
    toks = out.shape[0]
    for tok in range(toks):
        pieces = []
        for source in sources:
            inner = source.shape[1] // (outer * toks)
            values = source[...]
            for k in range(outer):
                start = (k * toks + tok) * inner
                pieces.append(values[:, start : start + inner])
        out[tok] = jnp.concatenate(pieces, axis=1)


def split_columns(weights, outer, toks):
    rows = weights[0].shape[0]
    cols = sum(w.shape[1] for w in weights) // toks
    return pl.pallas_call(
        functools.partial(split_kernel, outer),
        out_shape=jax.ShapeDtypeStruct((toks, rows, cols), weights[0].dtype),
        compiler_params=pltpu.CompilerParams(vmem_limit_bytes=32 * 2**20),
    )(*weights)


def join_kernel(outer, source, *outs):
    toks = source.shape[0]
    offset = 0
    for out in outs:
        inner = out.shape[1] // (outer * toks)
        pieces = []
        for k in range(outer):
            for tok in range(toks):
                start = offset + k * inner
                pieces.append(source[tok, :, start : start + inner].astype(f32))
        out[...] = jnp.concatenate(pieces, axis=1)
        offset += outer * inner


def join_columns(parts, outer, count):
    toks, rows, cols = parts.shape
    shape = jax.ShapeDtypeStruct((rows, toks * cols // count), f32)
    return pl.pallas_call(
        functools.partial(join_kernel, outer),
        out_shape=[shape] * count,
        compiler_params=pltpu.CompilerParams(vmem_limit_bytes=32 * 2**20),
    )(parts)


def body(
    tokens,
    cotangent,
    norm_gain,
    norm_bias,
    joint_weight,
    out_weight,
    gate_weight,
    up_weight,
    down_weight,
    block_table,
):
    grps, toks = lax.axis_size("grp"), lax.axis_size("tok")
    devices = grps * toks
    rows, width = tokens.shape
    own_heads = width // HD // toks
    span = own_heads * HD
    wide = gate_weight.shape[1] // toks
    tok = lax.axis_index("tok")

    pair = jnp.stack([norm_gain, norm_bias])
    pair = lax.all_to_all(jnp.broadcast_to(pair[None], (devices,) + pair.shape), both, 0, 0)
    gain = pair[:, 0].reshape(width).astype(f32)
    bias = pair[:, 1].reshape(width).astype(f32)

    tall = width // grps
    whole_heads = out_weight.shape[0] == HD and tall % QT == 0 and HD * grps % LANES == 0
    if whole_heads:
        first = gather_grp(jnp.concatenate([down_weight, out_weight]))
        first = first.reshape(grps, -1, width)
        down_w = first[:, : down_weight.shape[0]].reshape(-1, width)
        out_w = first[:, down_weight.shape[0] :].reshape(-1, width)
    else:
        down_w = first = gather_grp(down_weight)
        out_w = lax.all_gather(out_weight, both, axis=0, tiled=True)
        out_w = lax.dynamic_index_in_dim(
            out_w.reshape(own_heads, toks, HD, width), tok, 1, keepdims=False
        ).reshape(span, width)
    gate_up_own = swap_tok(split_columns([gate_weight, up_weight], grps, toks))
    gate_up_own = gate_up_own.reshape(-1, 2 * wide)
    own_tokens, gate_up_own, gain, bias = lax.optimization_barrier(
        (tokens, gate_up_own, gain, bias)
    )
    tables = rotary_tables()

    def with_tables(held):
        nonlocal tables
        held, tables = lax.optimization_barrier((held, tables))
        return held

    def with_hidden(held):
        nonlocal hidden
        held, hidden = lax.optimization_barrier((held, hidden))
        return held

    pieces, orders = gather_pieces(own_tokens, {2: with_tables})
    own_cotangent, pieces = lax.optimization_barrier((cotangent, pieces))
    hidden = assemble(pieces, gain[None], bias[None])
    slots = jnp.argsort(block_table[0] % BLK_GROUP).astype(jnp.int32)
    halves = len(orders)
    spots = [(tok ^ apart) * halves + half for apart, half in order_of(orders)]
    place = jnp.argsort(jnp.stack(spots))[slots].astype(jnp.int32)
    d_pieces, _ = gather_pieces(own_cotangent, {2: with_hidden})
    gate_up_w = gather_grp(after(gate_up_own, first))
    dy = assemble(d_pieces)
    d_attended = matmul_nt(dy, out_w).astype(bf16)
    joint_own = split_columns(
        [after(joint_weight, dy, d_attended, place)], 3 * own_heads, toks
    )
    joint_own = swap_tok(joint_own).reshape(-1, 3 * span)
    joint_w = gather_grp(after(joint_own, gate_up_w))

    activated, d_gate_up = feed_forward(hidden, dy, gate_up_w, down_w)
    gate_up_term = outer_product(hidden, d_gate_up)
    gate_up_grad = scatter_grp(after(gate_up_term, joint_w))

    joint = matmul(after(hidden, gate_up_term), joint_w)
    attended, d_joint = attention(place, joint, d_attended, tables)
    last = toks.bit_length() - 2
    flat = lambda pairs: [v for pair in pairs for v in pair]
    sums = sum_of_products([attended, activated], [out_w, down_w], False, halves)
    sums = scatter_step(sums, orders, last)
    d_joint_next = after(d_joint, *flat(sums))
    if whole_heads:
        head_term = head_terms(hidden, d_joint_next, attended, dy, grps)
    else:
        head_term = matmul_tn(hidden, d_joint_next).astype(bf16)
    head_sums = scatter_grp(after(head_term, gate_up_grad))
    gate_up_rows = swap_tok(after(gate_up_grad, head_term).reshape(toks, -1, 2 * wide))
    kept, gate_up_grad = lax.optimization_barrier(([pair[0] for pair in sums], gate_up_grad))
    sums = [(k, pair[1]) for k, pair in zip(kept, sums)]
    sums = scatter_step(sums, orders, last - 1)
    lefts = [after(d_joint, head_term, gate_up_grad, *flat(sums)), d_gate_up]
    d_sums = sum_of_products(lefts, [joint_w, gate_up_w], True, halves)
    d_sums, gate_up_rows = lax.optimization_barrier((d_sums, gate_up_rows))
    d_sums = scatter_step(d_sums, orders, last)
    down_term = matmul_tn(after(activated, *flat(d_sums)), dy).astype(bf16)
    d_sums = scatter_step(d_sums, orders, last - 1)
    d_sums, head_sums = lax.optimization_barrier((d_sums, head_sums))
    head_rows = head_sums[:, : 3 * span]
    head_rows = swap_tok(head_rows.reshape(toks, -1, 3 * span))
    kept, head_rows = lax.optimization_barrier(([pair[0] for pair in d_sums], head_rows))
    d_sums = [(k, pair[1]) for k, pair in zip(kept, d_sums)]
    for step in range(last - 2, -1, -1):
        d_sums = scatter_step(d_sums, orders, step)
    sums, head_rows = lax.optimization_barrier((sums, head_rows))
    for step in range(last - 2, -1, -1):
        sums = scatter_step(sums, orders, step)
    down_grad = scatter_grp(after(down_term, head_sums))
    d_hidden = jnp.concatenate(d_sums)
    result = (tokens.astype(f32) + jnp.concatenate(sums)).astype(bf16)
    if whole_heads:
        out_grad = head_sums[:, 3 * span :].reshape(tall // HD, HD, -1)
        out_grad = out_grad.transpose(1, 0, 2).reshape(HD, width).astype(f32)
    else:
        spread = jnp.zeros((own_heads, toks, HD, width), bf16)
        out_term = matmul_tn(attended, dy).astype(bf16).reshape(own_heads, 1, HD, width)
        spread = lax.dynamic_update_index_in_dim(spread, out_term, tok, 1)
        out_grad = lax.psum_scatter(
            spread.reshape(width, width), both, scatter_dimension=0, tiled=True
        ).astype(f32)
    tokens_wide = tokens.astype(f32)
    centred = tokens_wide - jnp.mean(tokens_wide, axis=-1, keepdims=True)
    inv_std = lax.rsqrt(jnp.mean(centred * centred, axis=-1, keepdims=True) + eps)
    normed = centred * inv_std
    d_normed = d_hidden * gain
    d_inputs = inv_std * (
        d_normed
        - jnp.mean(d_normed, axis=-1, keepdims=True)
        - normed * jnp.mean(d_normed * normed, axis=-1, keepdims=True)
    )
    input_grad = (cotangent.astype(f32) + d_inputs).astype(bf16)
    sums = jnp.stack([jnp.sum(d_hidden * normed, axis=0), jnp.sum(d_hidden, axis=0)])
    sums = lax.all_to_all(sums.reshape(2, devices, -1).transpose(1, 0, 2), both, 0, 0)
    sums, down_grad = lax.optimization_barrier((sums, down_grad.astype(f32)))
    sums = jnp.sum(sums, axis=0)

    return (
        result,
        input_grad,
        sums[0],
        sums[1],
        *join_columns(head_rows, 3 * own_heads, 1),
        out_grad,
        *join_columns(gate_up_rows, grps, 2),
        down_grad,
    )


def solution(mesh):
    sharded = P(("grp", "tok"), None)
    vector = P(("grp", "tok"))
    return jax.shard_map(
        body,
        mesh=mesh,
        in_specs=(sharded, sharded, vector, vector) + (sharded,) * 5 + (P("grp", None),),
        out_specs=(sharded, sharded, vector, vector) + (sharded,) * 5,
        check_vma=False,
    )
```

```python
import functools

import jax
import jax.numpy as jnp
from jax import lax
from jax.experimental import pallas as pl
from jax.experimental.pallas import tpu as pltpu
from jax.sharding import PartitionSpec as P

HD = 64
ROT = 16
BT = 128
PB = 8
BLK_GROUP = 16
LANES = 128
QT = 2 * BT

eps = 1e-05
neg_big = -1e30
bf16 = jnp.bfloat16
f32 = jnp.float32
both = ("grp", "tok")
no_cost = pl.CostEstimate(flops=0, transcendentals=0, bytes_accessed=0)


def matmul(left, right):
    return jnp.dot(left, right, preferred_element_type=f32)


def matmul_nt(left, right):
    return lax.dot_general(left, right, (((1,), (1,)), ((), ())), preferred_element_type=f32)


def matmul_tn(left, right):
    return lax.dot_general(left, right, (((0,), (0,)), ((), ())), preferred_element_type=f32)


def rotary_tables():
    positions = (PB + 1) * BT
    freq = 10000.0 ** (-jnp.arange(0, ROT, 2, dtype=f32) / ROT)
    angles = jnp.arange(positions, dtype=jnp.int32).astype(f32)[:, None] * freq[None, :]
    cosine, sine = jnp.cos(angles), jnp.sin(angles)
    rest = jnp.zeros((positions, HD - ROT), f32)
    none = jnp.zeros_like(sine)

    def widen(parts):
        one = jnp.concatenate(parts, axis=1)
        return jnp.concatenate([one] * (LANES // HD), axis=1)

    keep = widen([cosine, cosine, rest + 1.0])
    below = widen([-sine, none, rest])
    above = widen([none, sine, rest])
    return keep, below, above


def attention_kernel(
    place, joint, d_out, keep, below, above, out, d_joint, qs, ks, vs, ds, d_key, d_value
):
    span = d_out.shape[1]
    first = pl.program_id(0) * LANES
    lanes = [pl.ds(pl.multiple_of(c * span + first, LANES), LANES) for c in range(3)]

    def turned(values, part, sign):
        row = min(part, PB) * BT
        c, b, a = (t[row : row + BT, :] for t in (keep, below, above))
        up = pltpu.roll(values, LANES - ROT // 2, 1)
        down = pltpu.roll(values, ROT // 2, 1)
        return values * c + sign * (up * b + down * a)

    def rows_of(part):
        return pl.ds(pl.multiple_of(place[part] * BT, BT), BT)

    for part in range(BLK_GROUP):
        rows = rows_of(part)
        here = pl.ds(part * BT, BT)
        qs[here, :] = turned(joint[rows, lanes[0]], part, 1.0).astype(bf16) * HD ** (-0.5)
        ks[here, :] = turned(joint[rows, lanes[1]], part, 1.0).astype(bf16)
        vs[here, :] = joint[rows, lanes[2]].astype(bf16)
        ds[here, :] = d_out[rows, lanes[0]]

    row_id = lax.broadcasted_iota(jnp.int32, (QT, QT), 0)
    col_id = lax.broadcasted_iota(jnp.int32, (QT, QT), 1)
    causal = row_id >= col_id
    alone = causal & (row_id // BT == col_id // BT)
    head_of = lax.broadcasted_iota(jnp.int32, (QT, LANES), 1) // HD

    def one_head(head, own, shared, allowed):
        mine = head_of == head
        query = jnp.where(mine, qs[own, :], 0).astype(bf16)
        d_o = jnp.where(mine, ds[own, :], 0).astype(bf16)
        spans = [own] + ([pl.ds(0, shared)] if shared else [])
        raw = [matmul_nt(query, ks[s, :]) for s in spans]
        raw[0] = jnp.where(allowed, raw[0], neg_big)
        top = functools.reduce(jnp.maximum, [jnp.max(r, axis=1, keepdims=True) for r in raw])
        terms = [jnp.exp(r - top) for r in raw]
        total = functools.reduce(jnp.add, [jnp.sum(t, axis=1, keepdims=True) for t in terms])
        inverse = 1.0 / total
        weights = [t * inverse for t in terms]
        low = [w.astype(bf16) for w in weights]
        attended = functools.reduce(jnp.add, [matmul(w, vs[s, :]) for w, s in zip(low, spans)])
        delta = jnp.sum(attended * d_o.astype(f32), axis=1, keepdims=True)
        d_scores = [
            (w * (matmul_nt(d_o, vs[s, :]) - delta)).astype(bf16) for w, s in zip(weights, spans)
        ]
        d_query = functools.reduce(jnp.add, [matmul(d, ks[s, :]) for d, s in zip(d_scores, spans)])
        d_keys = [matmul_tn(d, query) for d in d_scores]
        d_values = [matmul_tn(w, d_o) for w in low]
        return attended, d_query, d_keys, d_values

    def tile(index, shared, allowed):
        own = pl.ds(index * QT, QT)
        found = [one_head(head, own, shared, allowed) for head in range(LANES // HD)]
        attended, d_query = found[0][:2]
        for head in range(1, LANES // HD):
            mine = head_of == head
            attended = jnp.where(mine, found[head][0], attended)
            d_query = jnp.where(mine, found[head][1], d_query)
        d_query = d_query * HD ** (-0.5)
        d_keys, d_values = (
            [functools.reduce(jnp.add, parts) for parts in zip(*(f[k] for f in found))]
            for k in (2, 3)
        )
        d_key[own, :] = d_keys[0]
        d_value[own, :] = d_values[0]
        if shared:
            d_key[:shared, :] += d_keys[1]
            d_value[:shared, :] += d_values[1]
        for k in range(QT // BT):
            part = index * (QT // BT) + k
            rows = rows_of(part)
            piece = slice(k * BT, (k + 1) * BT)
            out[rows, lanes[0]] = attended[piece, :].astype(bf16)
            d_joint[rows, lanes[0]] = turned(d_query[piece, :], part, -1.0).astype(bf16)

    prompt_tiles = PB * BT // QT
    for index in range(BLK_GROUP * BT // QT):
        if index < prompt_tiles:
            tile(index, index * QT, causal)
        else:
            tile(index, PB * BT, alone)
    for part in range(BLK_GROUP):
        here = pl.ds(part * BT, BT)
        rows = rows_of(part)
        d_joint[rows, lanes[1]] = turned(d_key[here, :], part, -1.0).astype(bf16)
        d_joint[rows, lanes[2]] = d_value[here, :].astype(bf16)


def attention(place, joint, d_out, tables):
    count, span = d_out.shape
    full = lambda shape: pl.BlockSpec(shape, lambda h, p: (0,) * len(shape))
    scratch = [pltpu.VMEM((count, LANES), bf16)] * 4 + [pltpu.VMEM((count, LANES), f32)] * 2
    return pl.pallas_call(
        attention_kernel,
        grid_spec=pltpu.PrefetchScalarGridSpec(
            num_scalar_prefetch=1,
            grid=(span // LANES,),
            in_specs=[full(joint.shape), full(d_out.shape)] + [full(t.shape) for t in tables],
            out_specs=[full((count, span)), full((count, 3 * span))],
            scratch_shapes=scratch,
        ),
        out_shape=[
            jax.ShapeDtypeStruct((count, span), bf16),
            jax.ShapeDtypeStruct((count, 3 * span), bf16),
        ],
        compiler_params=pltpu.CompilerParams(vmem_limit_bytes=48 * 2**20),
        cost_estimate=no_cost,
    )(place, joint, d_out, *tables)


def after(values, *earlier):
    return lax.optimization_barrier((values, earlier))[0]


def gather_pieces(values, between):
    toks = lax.axis_size("tok")
    bits = toks.bit_length() - 1
    paths = values.shape[0] // BT
    orders = [list(range(1, bits)) + [0], list(range(bits - 1, 0, -1)) + [0]]
    held = list(jnp.split(values, paths))
    found = []
    for step in range(bits):
        if step in between:
            held = between[step](held)
        swaps = [[(i, i ^ (1 << orders[p % 2][step])) for i in range(toks)] for p in range(paths)]
        got = [lax.ppermute(h, "tok", s) for h, s in zip(held, swaps)]
        if step == bits - 1:
            found = [piece for pair in zip(held, got) for piece in pair]
        else:
            held = [jnp.concatenate(pair) for pair in zip(held, got)]
    return found, orders[:paths]


def order_of(orders):
    found = []
    for half, order in enumerate(orders):
        for q in range(1 << len(order)):
            found.append((sum(1 << b for k, b in enumerate(order) if q >> k & 1), half))
    return found


def assemble_kernel(count, norm, *refs):
    pieces, refs = refs[:count], refs[count:]
    step = pl.program_id(0)
    each = pl.num_programs(0) // count
    for k, piece in enumerate(pieces):

        @pl.when(step // each == k)
        def _():
            if norm:
                gain, bias, out = refs
                values = piece[...].astype(f32)
                centred = values - jnp.mean(values, axis=-1, keepdims=True)
                spread = jnp.mean(centred * centred, axis=-1, keepdims=True)
                out[...] = (centred * lax.rsqrt(spread + eps) * gain[...] + bias[...]).astype(bf16)
            else:
                refs[-1][...] = piece[...]


def assemble(pieces, *norm):
    tall, width = pieces[0].shape
    block = min(tall, QT)
    each = tall // block
    total = tall * len(pieces)

    def piece_block(k):
        return pl.BlockSpec((block, width), lambda i: (jnp.clip(i - k * each, 0, each - 1), 0))

    return pl.pallas_call(
        functools.partial(assemble_kernel, len(pieces), bool(norm)),
        grid=(total // block,),
        in_specs=[piece_block(k) for k in range(len(pieces))]
        + [pl.BlockSpec((1, width), lambda i: (0, 0)) for _ in norm],
        out_specs=pl.BlockSpec((block, width), lambda i: (i, 0)),
        out_shape=jax.ShapeDtypeStruct((total, width), bf16),
        compiler_params=pltpu.CompilerParams(vmem_limit_bytes=48 * 2**20),
        cost_estimate=pl.CostEstimate(
            flops=10 * total * width, transcendentals=0, bytes_accessed=8 * total * width
        ),
    )(*pieces, *norm)


def sum_kernel(count, transposed, *refs):
    product = matmul_nt if transposed else matmul
    terms = [product(refs[k][...], refs[count + k][...]) for k in range(count)]
    total = functools.reduce(jnp.add, terms).astype(bf16)
    outs = refs[2 * count :]
    each = pl.num_programs(0) // len(outs)
    for k, out in enumerate(outs):

        @pl.when(pl.program_id(0) // each == k)
        def _():
            out[...] = total


def sum_of_products(lefts, rights, transposed, paths):
    rows = lefts[0].shape[0]
    cols = rights[0].shape[0 if transposed else 1]
    outs = 2 * paths
    each = rows // outs // QT

    def left_block(i):
        which = i // each
        return (which % paths * 2 * each + (1 - which // paths) * each + i % each, 0)

    def out_block(k):
        return pl.BlockSpec((QT, cols), lambda i: (jnp.clip(i - k * each, 0, each - 1), 0))

    found = pl.pallas_call(
        functools.partial(sum_kernel, len(lefts), transposed),
        grid=(rows // QT,),
        in_specs=[pl.BlockSpec((QT, v.shape[1]), left_block) for v in lefts]
        + [pl.BlockSpec(v.shape, lambda i: (0, 0), pipeline_mode=pl.Buffered(1)) for v in rights],
        out_specs=[out_block(k) for k in range(outs)],
        out_shape=[jax.ShapeDtypeStruct((rows // outs, cols), bf16)] * outs,
        compiler_params=pltpu.CompilerParams(vmem_limit_bytes=48 * 2**20),
        cost_estimate=(pl.CostEstimate(flops=18*10**9, transcendentals=0, bytes_accessed=10**7) if transposed else no_cost),
    )(*lefts, *rights)
    return list(zip(found[paths:], found[:paths]))


def feed_kernel(hidden, d_result, up_weight, down_weight, act, d_both):
    wide = act.shape[1]
    both_here = matmul(hidden[...], up_weight[...])
    d_act = matmul_nt(d_result[...], down_weight[...])
    gate, up = both_here[:, :wide], both_here[:, wide:]
    sigma = jax.nn.sigmoid(gate)
    swish = gate * sigma
    act[...] = (swish * up).astype(bf16)
    d_gate = d_act * up * sigma * (1.0 + gate * (1.0 - sigma))
    d_both[...] = jnp.concatenate([d_gate, d_act * swish], axis=1).astype(bf16)


def feed_forward(hidden, d_result, up_weight, down_weight):
    rows, width = hidden.shape
    wide = down_weight.shape[0]
    fixed = lambda w: pl.BlockSpec(w.shape, lambda i: (0, 0), pipeline_mode=pl.Buffered(1))
    return pl.pallas_call(
        feed_kernel,
        grid=(rows // QT,),
        in_specs=[pl.BlockSpec((QT, width), lambda i: (i, 0))] * 2
        + [fixed(up_weight), fixed(down_weight)],
        out_specs=[
            pl.BlockSpec((QT, wide), lambda i: (i, 0)),
            pl.BlockSpec((QT, 2 * wide), lambda i: (i, 0)),
        ],
        out_shape=[
            jax.ShapeDtypeStruct((rows, wide), bf16),
            jax.ShapeDtypeStruct((rows, 2 * wide), bf16),
        ],
        compiler_params=pltpu.CompilerParams(vmem_limit_bytes=48 * 2**20),
        cost_estimate=no_cost,
    )(hidden, d_result, up_weight, down_weight)


def outer_kernel(left, right, out):
    out[...] = matmul_tn(left[...], right[...]).astype(bf16)


def outer_product(left, right):
    rows, tall = left.shape
    wide = right.shape[1]
    return pl.pallas_call(
        outer_kernel,
        grid=(tall // QT,),
        in_specs=[
            pl.BlockSpec((rows, QT), lambda i: (0, i)),
            pl.BlockSpec((rows, wide), lambda i: (0, 0), pipeline_mode=pl.Buffered(1)),
        ],
        out_specs=pl.BlockSpec((QT, wide), lambda i: (i, 0)),
        out_shape=jax.ShapeDtypeStruct((tall, wide), bf16),
        compiler_params=pltpu.CompilerParams(vmem_limit_bytes=48 * 2**20),
        cost_estimate=no_cost,
    )(left, right)


def scatter_step(pairs, orders, step):
    toks = lax.axis_size("tok")
    held = []
    for (kept, sent), order in zip(pairs, orders):
        got = lax.ppermute(sent, "tok", [(i, i ^ (1 << order[step])) for i in range(toks)])
        held.append(kept.astype(f32) + got.astype(f32))
    if not step:
        return held
    tall = held[0].shape[0] // 2
    return lax.optimization_barrier(
        [(h[:tall].astype(bf16), h[tall:].astype(bf16)) for h in held]
    )


def head_terms_kernel(tall, hidden, d_joint, attended, d_result, out):
    grps = pl.num_programs(0) // (tall // QT)
    upper = pl.program_id(0) % grps % (LANES // HD) != 0
    split = d_joint.shape[1]
    out[:, :split] = matmul_tn(hidden[...], d_joint[...]).astype(bf16)
    term = matmul_tn(attended[...], d_result[...])
    term = jnp.where(upper, term[HD:], term[:HD]).astype(bf16)
    wide = out.shape[1] - split
    for k in range(QT // HD):
        out[k * HD : (k + 1) * HD, split:] = term[:, k * wide : (k + 1) * wide]


def head_terms(hidden, d_joint, attended, d_result, grps):
    rows, width = hidden.shape
    tall = width // grps
    each = tall // QT
    wide = HD * width // tall
    return pl.pallas_call(
        functools.partial(head_terms_kernel, tall),
        grid=(each * grps,),
        in_specs=[
            pl.BlockSpec((rows, QT), lambda i: (0, i % grps * each + i // grps)),
            pl.BlockSpec(d_joint.shape, lambda i: (0, 0), pipeline_mode=pl.Buffered(1)),
            pl.BlockSpec((rows, LANES), lambda i: (0, i % grps // (LANES // HD))),
            pl.BlockSpec((rows, width // each), lambda i: (0, i // grps)),
        ],
        out_specs=pl.BlockSpec(
            (QT, d_joint.shape[1] + wide), lambda i: (i % grps * each + i // grps, 0)
        ),
        out_shape=jax.ShapeDtypeStruct((width, d_joint.shape[1] + wide), bf16),
        compiler_params=pltpu.CompilerParams(vmem_limit_bytes=48 * 2**20),
        cost_estimate=no_cost,
    )(hidden, d_joint, attended, d_result)


def gather_grp(values):
    return lax.all_gather(values, "grp", axis=0, tiled=True)


def scatter_grp(values):
    return lax.psum_scatter(values.astype(bf16), "grp", scatter_dimension=0, tiled=True)


def swap_tok(values):
    return lax.all_to_all(values, "tok", 0, 0)


def split_kernel(outer, *refs):
    sources, out = refs[:-1], refs[-1]
    toks = out.shape[0]
    for tok in range(toks):
        pieces = []
        for source in sources:
            inner = source.shape[1] // (outer * toks)
            values = source[...]
            for k in range(outer):
                start = (k * toks + tok) * inner
                pieces.append(values[:, start : start + inner])
        out[tok] = jnp.concatenate(pieces, axis=1)


def split_columns(weights, outer, toks):
    rows = weights[0].shape[0]
    cols = sum(w.shape[1] for w in weights) // toks
    return pl.pallas_call(
        functools.partial(split_kernel, outer),
        out_shape=jax.ShapeDtypeStruct((toks, rows, cols), weights[0].dtype),
        compiler_params=pltpu.CompilerParams(vmem_limit_bytes=32 * 2**20),
    )(*weights)


def join_kernel(outer, source, *outs):
    toks = source.shape[0]
    offset = 0
    for out in outs:
        inner = out.shape[1] // (outer * toks)
        pieces = []
        for k in range(outer):
            for tok in range(toks):
                start = offset + k * inner
                pieces.append(source[tok, :, start : start + inner].astype(f32))
        out[...] = jnp.concatenate(pieces, axis=1)
        offset += outer * inner


def join_columns(parts, outer, count):
    toks, rows, cols = parts.shape
    shape = jax.ShapeDtypeStruct((rows, toks * cols // count), f32)
    return pl.pallas_call(
        functools.partial(join_kernel, outer),
        out_shape=[shape] * count,
        compiler_params=pltpu.CompilerParams(vmem_limit_bytes=32 * 2**20),
    )(parts)


def body(
    tokens,
    cotangent,
    norm_gain,
    norm_bias,
    joint_weight,
    out_weight,
    gate_weight,
    up_weight,
    down_weight,
    block_table,
):
    grps, toks = lax.axis_size("grp"), lax.axis_size("tok")
    devices = grps * toks
    rows, width = tokens.shape
    own_heads = width // HD // toks
    span = own_heads * HD
    wide = gate_weight.shape[1] // toks
    tok = lax.axis_index("tok")

    pair = jnp.stack([norm_gain, norm_bias])
    pair = lax.all_to_all(jnp.broadcast_to(pair[None], (devices,) + pair.shape), both, 0, 0)
    gain = pair[:, 0].reshape(width).astype(f32)
    bias = pair[:, 1].reshape(width).astype(f32)

    tall = width // grps
    whole_heads = out_weight.shape[0] == HD and tall % QT == 0 and HD * grps % LANES == 0
    if whole_heads:
        first = gather_grp(jnp.concatenate([down_weight, out_weight]))
        first = first.reshape(grps, -1, width)
        down_w = first[:, : down_weight.shape[0]].reshape(-1, width)
        out_w = first[:, down_weight.shape[0] :].reshape(-1, width)
    else:
        down_w = first = gather_grp(down_weight)
        out_w = lax.all_gather(out_weight, both, axis=0, tiled=True)
        out_w = lax.dynamic_index_in_dim(
            out_w.reshape(own_heads, toks, HD, width), tok, 1, keepdims=False
        ).reshape(span, width)
    gate_up_own = swap_tok(split_columns([gate_weight, up_weight], grps, toks))
    gate_up_own = gate_up_own.reshape(-1, 2 * wide)
    own_tokens, gate_up_own, gain, bias = lax.optimization_barrier(
        (tokens, gate_up_own, gain, bias)
    )
    tables = rotary_tables()

    def with_tables(held):
        nonlocal tables
        held, tables = lax.optimization_barrier((held, tables))
        return held

    def with_hidden(held):
        nonlocal hidden
        held, hidden = lax.optimization_barrier((held, hidden))
        return held

    pieces, orders = gather_pieces(own_tokens, {2: with_tables})
    own_cotangent, pieces = lax.optimization_barrier((cotangent, pieces))
    hidden = assemble(pieces, gain[None], bias[None])
    slots = jnp.argsort(block_table[0] % BLK_GROUP).astype(jnp.int32)
    halves = len(orders)
    spots = [(tok ^ apart) * halves + half for apart, half in order_of(orders)]
    place = jnp.argsort(jnp.stack(spots))[slots].astype(jnp.int32)
    d_pieces, _ = gather_pieces(own_cotangent, {2: with_hidden})
    gate_up_w = gather_grp(after(gate_up_own, first))
    dy = assemble(d_pieces)
    d_attended = matmul_nt(dy, out_w).astype(bf16)
    joint_own = split_columns(
        [after(joint_weight, dy, d_attended, place)], 3 * own_heads, toks
    )
    joint_own = swap_tok(joint_own).reshape(-1, 3 * span)
    joint_w = gather_grp(after(joint_own, gate_up_w))

    activated, d_gate_up = feed_forward(hidden, dy, gate_up_w, down_w)
    gate_up_term = outer_product(hidden, d_gate_up)
    gate_up_grad = scatter_grp(after(gate_up_term, joint_w))

    joint = matmul(after(hidden, gate_up_term), joint_w)
    attended, d_joint = attention(place, joint, d_attended, tables)
    last = toks.bit_length() - 2
    if whole_heads:
        head_sums = head_terms(hidden, d_joint, attended, dy, grps)
    else:
        head_sums = matmul_tn(hidden, d_joint).astype(bf16)
    flat = lambda pairs: [v for pair in pairs for v in pair]
    lefts = [after(attended, head_sums), activated]
    sums = sum_of_products(lefts, [out_w, down_w], False, halves)
    head_sums = scatter_grp(after(head_sums, gate_up_grad))
    sums = scatter_step(sums, orders, last)
    gate_up_rows = swap_tok(after(gate_up_grad, *flat(sums)).reshape(toks, -1, 2 * wide))
    lefts = [after(d_joint, *flat(sums)), d_gate_up]
    d_sums = sum_of_products(lefts, [joint_w, gate_up_w], True, halves)
    d_sums, gate_up_rows = lax.optimization_barrier((d_sums, gate_up_rows))
    sums = scatter_step(sums, orders, last - 1)
    d_sums = scatter_step(d_sums, orders, last)
    d_sums, sums = lax.optimization_barrier((d_sums, sums))
    down_term = matmul_tn(after(activated, *flat(d_sums)), dy).astype(bf16)
    kept, head_sums = lax.optimization_barrier(([pair[0] for pair in d_sums], head_sums))
    d_sums = [(k, pair[1]) for k, pair in zip(kept, d_sums)]
    d_sums = scatter_step(d_sums, orders, last - 1)
    head_rows = after(head_sums[:, : 3 * span], *flat(d_sums))
    head_rows = swap_tok(head_rows.reshape(toks, -1, 3 * span))
    kept, head_rows = lax.optimization_barrier(([pair[0] for pair in d_sums], head_rows))
    d_sums = [(k, pair[1]) for k, pair in zip(kept, d_sums)]
    for step in range(last - 2, -1, -1):
        d_sums = scatter_step(d_sums, orders, step)
    sums, head_rows = lax.optimization_barrier((sums, head_rows))
    for step in range(last - 2, -1, -1):
        sums = scatter_step(sums, orders, step)
    down_grad = scatter_grp(after(down_term, head_sums))
    d_hidden = jnp.concatenate(d_sums)
    result = (tokens.astype(f32) + jnp.concatenate(sums)).astype(bf16)
    if whole_heads:
        out_grad = head_sums[:, 3 * span :].reshape(tall // HD, HD, -1)
        out_grad = out_grad.transpose(1, 0, 2).reshape(HD, width).astype(f32)
    else:
        spread = jnp.zeros((own_heads, toks, HD, width), bf16)
        out_term = matmul_tn(attended, dy).astype(bf16).reshape(own_heads, 1, HD, width)
        spread = lax.dynamic_update_index_in_dim(spread, out_term, tok, 1)
        out_grad = lax.psum_scatter(
            spread.reshape(width, width), both, scatter_dimension=0, tiled=True
        ).astype(f32)
    tokens_wide = tokens.astype(f32)
    centred = tokens_wide - jnp.mean(tokens_wide, axis=-1, keepdims=True)
    inv_std = lax.rsqrt(jnp.mean(centred * centred, axis=-1, keepdims=True) + eps)
    normed = centred * inv_std
    d_normed = d_hidden * gain
    d_inputs = inv_std * (
        d_normed
        - jnp.mean(d_normed, axis=-1, keepdims=True)
        - normed * jnp.mean(d_normed * normed, axis=-1, keepdims=True)
    )
    input_grad = (cotangent.astype(f32) + d_inputs).astype(bf16)
    sums = jnp.stack([jnp.sum(d_hidden * normed, axis=0), jnp.sum(d_hidden, axis=0)])
    sums = lax.all_to_all(sums.reshape(2, devices, -1).transpose(1, 0, 2), both, 0, 0)
    sums = jnp.sum(sums, axis=0)

    return (
        result,
        input_grad,
        sums[0],
        sums[1],
        *join_columns(head_rows, 3 * own_heads, 1),
        out_grad,
        *join_columns(gate_up_rows, grps, 2),
        down_grad.astype(f32),
    )


def solution(mesh):
    sharded = P(("grp", "tok"), None)
    vector = P(("grp", "tok"))
    return jax.shard_map(
        body,
        mesh=mesh,
        in_specs=(sharded, sharded, vector, vector) + (sharded,) * 5 + (P("grp", None),),
        out_specs=(sharded, sharded, vector, vector) + (sharded,) * 5,
        check_vma=False,
    )
```
